128 devices in a mesh: lead: 2 (over z_hi), tile: 64 (over y, z_lo, x, core).
Axes of the slice: x: 4, y: 4, z: 4 (z_hi: 2, z_lo: 2; z = z_hi * 2 + z_lo), core: 2. Of those that a mesh axis runs over, the one named last changes fastest.
Arguments:
- states: float32 [2, 2, 128, 512, 128], P('lead', None, None, 'tile'), may hold values from -6 to 6
- cotangents: float32 [2, 2, 128, 512, 128], P('lead', None, None, 'tile'), may hold values from -6 to 6
- w_conv: bfloat16 [1152, 512], replicated, may hold values from -0.1875 to 0.1875
- b_conv: float32 [512], replicated, may hold values from -3 to 3
- w_out: bfloat16 [512, 128], replicated, may hold values from -0.25 to 0.25
- forcing: float32 [365, 128], replicated, may hold values from -3 to 3
- land: int32 [512, 128], P('tile'), may hold values 0 or 1
- dates: int32 [2], replicated, may hold values from 0 to 364
Outputs:
- state_grads: float32 [2, 2, 128, 512, 128], P('lead', None, None, 'tile')
- w1_grad: float32 [1152, 512], P('tile')
- w2_grad: float32 [512, 128], P('tile')
- b1_grad: float32 [512], P('tile')
The draws below stay inside these ranges and needn't reach their ends.
Inputs may be any that keep to these rules, and one draw needn't show every extreme that they name: 1 marks an ocean column, 0 a land column.
All inputs are finite; a program needn't handle non-finite values. No bound on the sum of `land` on one device may be relied on, other than what follows from the above.
Results may differ from the reference program's by a relative error of at most 0.0056.
Values may be sent and summed in bfloat16 or wider, within the bound.
A program may use at most 128 MiB of HBM per device.

```python
import math
import jax
import jax.numpy as jnp
from jax import lax

C = 128
H = 512
DAYS = 365
NX = 128
MB = 2
NY = 512
N_LEAD = 2


def place_ends(array, key, least, largest):
    index_at = [jax.random.randint(jax.random.fold_in(key, axis), (), 0, length) for axis, length in enumerate(array.shape)]
    main_axis = array.shape.index(max(array.shape))
    next_to = index_at[:main_axis] + [(index_at[main_axis] + 1) % array.shape[main_axis]] + index_at[main_axis + 1:]
    return array.at[tuple(index_at)].set(least).at[tuple(next_to)].set(largest)


def level_of(own_key, extent, cuts, least, top_value):
    def one(dim, parts):
        heights = jax.random.uniform(jax.random.fold_in(jax.random.fold_in(own_key, 6), dim), (parts,), jnp.float32, least / len(cuts), top_value / len(cuts))
        return jnp.repeat(jnp.exp(heights), extent[dim] // parts).reshape((-1,) + (1,) * (len(extent) - dim - 1))

    level = one(*cuts[0])
    for cut in cuts[1:]:
        level = level * one(*cut)
    return level


def normal_values(rng, extent, spread, reach, split=(), kind=jnp.bfloat16):
    drawn = jax.random.normal(rng, extent, jnp.float32) * spread
    if len(split) > 0:
        drawn = level_of(rng, extent, split, -0.22, 0.18) * drawn
    return jnp.clip(drawn, min=-reach, max=reach).astype(kind)


def setup_inputs(seed: int = 0) -> dict:
    key_list = jax.random.split(jax.random.key(seed), 9)
    return {
        "states": normal_values(key_list[0], (N_LEAD, MB, C, NY, NX), 1.0, 6.0, ((0, 2), (3, 64)), jnp.float32),
        "cotangents": normal_values(key_list[1], (N_LEAD, MB, C, NY, NX), 1.0, 6.0, ((0, 2), (3, 64)), jnp.float32),
        "w_conv": normal_values(key_list[2], (9 * C, H), (9 * C) ** -0.5, 0.1875),
        "b_conv": normal_values(key_list[3], (H,), 0.5, 3.0, (), jnp.float32),
        "w_out": normal_values(key_list[4], (H, C), H ** -0.5, 0.25),
        "forcing": normal_values(key_list[5], (DAYS, C), 0.5, 3.0, (), jnp.float32),
        "land": place_ends((jax.random.randint(key_list[6], (NY, NX), 0, 10) < 7).astype(jnp.int32), jax.random.fold_in(key_list[6], 1), 0, 1),
        "dates": jax.random.randint(key_list[7], (MB,), 0, DAYS).astype(jnp.int32),
    }


TANH_SCALE = 0.7978845608028654
CUBIC_TERM = 0.044715
OFFSETS = [(-1, -1), (-1, 0), (-1, 1), (0, -1), (0, 0), (0, 1), (1, -1), (1, 0), (1, 1)]

def gelu_pair(values):
    tanh_value = jnp.tanh(TANH_SCALE * (values + CUBIC_TERM * values * values * values))
    output = 0.5 * values * (1.0 + tanh_value)
    gelu_slope = 0.5 * (1.0 + tanh_value) + 0.5 * values * (1.0 - tanh_value * tanh_value) * TANH_SCALE * (1.0 + 3.0 * CUBIC_TERM * values * values)
    return (output, gelu_slope)

def matmul_full(left, right):
    return jnp.dot(left.astype(jnp.float32), right.astype(jnp.float32), precision=lax.Precision.HIGHEST, preferred_element_type=jnp.float32)

def member_grad(state_field, total_grad, shift_row, w_conv, b_conv, w_out, land_cols):
    channels, lat_rows, lon_cols = state_field.shape
    hidden_width = w_conv.shape[1]
    columns = lat_rows * lon_cols
    rounded = (state_field + shift_row[:, None, None]).astype(jnp.bfloat16)
    padded = jnp.pad(rounded, ((0, 0), (1, 1), (0, 0)))
    preact = jnp.zeros((hidden_width, columns), jnp.float32) + b_conv[:, None]
    tap_views = []
    for offset, (row_step, col_step) in enumerate(OFFSETS):
        tap_view = jnp.roll(padded[:, 1 + row_step:1 + row_step + lat_rows, :], -col_step, axis=2).reshape(channels, columns)
        tap_views.append(tap_view)
        tap_block = w_conv[offset * channels:(offset + 1) * channels]
        preact = preact + matmul_full(tap_block.T, tap_view)
    output, gelu_slope = gelu_pair(preact)
    hidden = output.astype(jnp.bfloat16)
    masked = (land_cols[None] * total_grad).astype(jnp.bfloat16).reshape(channels, columns)
    hidden_grad = matmul_full(w_out, masked)
    pre_grad = hidden_grad * gelu_slope
    pre_round = pre_grad.astype(jnp.bfloat16)
    w2_part = matmul_full(hidden, masked.T)
    bias_part = lax.optimization_barrier(jnp.sum(pre_grad, axis=1))
    w1_part = jnp.concatenate([matmul_full(tap_view, pre_round.T) for tap_view in tap_views], axis=0)
    input_grad = jnp.zeros((channels, lat_rows, lon_cols), jnp.float32)
    for offset, (row_step, col_step) in enumerate(OFFSETS):
        tap_block = w_conv[offset * channels:(offset + 1) * channels]
        tap_term = matmul_full(tap_block, pre_round).reshape(channels, lat_rows, lon_cols)
        tap_term = jnp.pad(tap_term, ((0, 0), (1, 1), (0, 0)))
        input_grad = input_grad + jnp.roll(tap_term[:, 1 - row_step:1 - row_step + lat_rows, :], col_step, axis=2)
    return (total_grad + input_grad, w1_part, w2_part, bias_part)

def reference(states, cotangents, w_conv, b_conv, w_out, forcing, land, dates):
    section_count = states.shape[0]
    member_count = states.shape[1]
    day_count = forcing.shape[0]
    land_cols = land.astype(jnp.float32)
    w1_total = jnp.zeros(w_conv.shape, jnp.float32)
    w2_total = jnp.zeros(w_out.shape, jnp.float32)
    bias_total = jnp.zeros(b_conv.shape, jnp.float32)
    incoming = jnp.zeros(states.shape[1:], jnp.float32)
    results = [None] * section_count
    for section_index in reversed(range(section_count)):
        day_index = ((dates + section_index) % day_count).astype(jnp.int32)
        picked = (jnp.arange(day_count, dtype=jnp.int32)[None, :] == day_index[:, None]).astype(jnp.float32)
        shifts = jnp.dot(picked, forcing, precision=lax.Precision.HIGHEST, preferred_element_type=jnp.float32)
        totals = cotangents[section_index] + incoming
        member_list = []
        for member in range(member_count):
            member_grads, w1_part, w2_part, bias_part = member_grad(states[section_index, member], totals[member], shifts[member], w_conv, b_conv, w_out, land_cols)
            member_list.append(member_grads)
            w1_total = w1_total + w1_part
            w2_total = w2_total + w2_part
            bias_total = bias_total + bias_part
        results[section_index] = jnp.stack(member_list)
        incoming = results[section_index]
    grad_scale = 1.0 / math.sqrt(section_count * member_count * land.shape[0] * land.shape[1])
    return (jnp.stack(results), w1_total * grad_scale, w2_total * grad_scale, bias_total * grad_scale)
```

```python
import functools
import math

import jax
import jax.numpy as jnp
from jax import lax
from jax.experimental import pallas as pl
from jax.experimental.pallas import tpu as pltpu
from jax.sharding import PartitionSpec as P

MESH = pl.DeviceIdType.MESH
TANH_SCALE = 0.7978845608028654
CUBIC_TERM = 0.044715
F32 = jnp.float32
BF16 = jnp.bfloat16

C = 128
H = 512
ROWS = 8
L = 128
MB = 2
TILES = 64
BLOCKS = 8
LOCAL = 8
BROWS = 176


def remote(src, dst, send_sem, recv_sem, device):
    return pltpu.make_async_remote_copy(
        src_ref=src, dst_ref=dst, send_sem=send_sem, recv_sem=recv_sem,
        device_id=device, device_id_type=MESH,
    )


def dot(a, b):
    return jnp.dot(a, b, preferred_element_type=F32)


def dot_t(a, b):
    return lax.dot_general(a, b, (((1,), (1,)), ((), ())), preferred_element_type=F32)


def rolled(value, shift):
    return value if shift % L == 0 else pltpu.roll(value, shift % L, 1)


def kernel(
    scale,
    dates, x_hbm, cot_hbm, w_hbm, b_hbm, wo_hbm, f_hbm, land_hbm,
    out_hbm, w1_out, w2_out, b1_out,
    x_v, cot_v, w_v, wt_v, b_v, wo_v, f_v, land_v,
    bcol, shift, taps, halo_s, halo_r, hidden, slope, masked, pre, bias_acc,
    edge_s, edge_r, part, sg_s, sg_r, out_v, w1_acc, w2_acc, b_row,
    c_s, c_r, y_s, y_r, y_sum, f_s, f_r, l_s, l_r,
    in_sem, out_sem, halo_ss, halo_rs, edge_ss, edge_rs, sg_ss, sg_rs,
    c_ss, c_rs, y_ss, y_rs, f_ss, f_rs, l_ss, l_rs,
):
    lead = lax.axis_index("lead")
    tile = lax.axis_index("tile")
    core = lax.rem(tile, 2)
    local = lax.rem(tile, LOCAL)
    block = lax.div(tile, LOCAL)
    xpos = lax.div(local, 2)

    peers = [(lead, lax.rem(tile + 1, TILES)), (lead, lax.rem(tile + TILES - 1, TILES)), (1 - lead, tile)]
    peers += [(lead, lax.rem(block + k, BLOCKS) * LOCAL + local) for k in range(1, BLOCKS)]
    peers += [(lead, block * LOCAL + lax.rem(local + k, LOCAL)) for k in range(1, LOCAL)]
    barrier = pltpu.get_barrier_semaphore()
    for peer in peers:
        pl.semaphore_signal(barrier, inc=1, device_id=peer, device_id_type=MESH)

    loads = [
        pltpu.make_async_copy(src, dst, in_sem.at[i])
        for i, (src, dst) in enumerate(
            [(f_hbm, f_v), (x_hbm, x_v), (w_hbm, w_v), (b_hbm, b_v), (cot_hbm, cot_v), (land_hbm, land_v), (wo_hbm, wo_v)]
        )
    ]
    for load in loads:
        load.start()

    loads[0].wait()
    for m in range(MB):
        day = lax.rem(dates[m] + lead, f_hbm.shape[0])
        shift[m] = jnp.broadcast_to(f_v[pl.ds(day, 1), :], (C, L)).T
    loads[1].wait()
    for m in range(MB):
        for d, r in ((0, 0), (1, ROWS - 1)):
            halo_s[d, m] = (x_v[m, pl.ds(r, C, stride=ROWS), :] + shift[m]).astype(BF16)
    pl.semaphore_wait(barrier, len(peers))
    halo_up = remote(halo_s.at[0], halo_r.at[1], halo_ss.at[0], halo_rs.at[1], (lead, tile - 1))
    halo_down = remote(halo_s.at[1], halo_r.at[0], halo_ss.at[1], halo_rs.at[0], (lead, tile + 1))

    @pl.when(tile > 0)
    def _():
        halo_up.start()

    @pl.when(tile < TILES - 1)
    def _():
        halo_down.start()

    @pl.when(tile == 0)
    def _():
        halo_r[0] = jnp.zeros_like(halo_r[0])

    @pl.when(tile == TILES - 1)
    def _():
        halo_r[1] = jnp.zeros_like(halo_r[1])

    for m in range(MB):
        for r in range(ROWS):
            rounded = (x_v[m, pl.ds(r, C, stride=ROWS), :] + shift[m])
            for cs in (-1, 0, 1):
                view = rolled(rounded, -cs).astype(BF16)
                for rs in (-1, 0, 1):
                    if 0 <= r - rs < ROWS:
                        tap = 3 * (rs + 1) + cs + 1
                        taps[m, tap * C:(tap + 1) * C, (r - rs) * L:(r - rs + 1) * L] = view

    loads[2].wait()
    for i in range(9):
        for j in range(4):
            wt_v[j * 128:(j + 1) * 128, i * 128:(i + 1) * 128] = w_v[i * 128:(i + 1) * 128, j * 128:(j + 1) * 128].T
    loads[3].wait()
    for j in range(4):
        bcol[j * 128:(j + 1) * 128, :] = jnp.broadcast_to(b_v[:, j * 128:(j + 1) * 128], (L, L)).T
    pre[...] = jnp.zeros_like(pre)
    bias_acc[...] = jnp.zeros_like(bias_acc)

    @pl.when(lead == 1)
    def _():
        sg_r[...] = jnp.zeros_like(sg_r)

    for load in loads[4:]:
        load.wait()

    def halo_arrived():
        @pl.when(tile > 0)
        def _():
            halo_down.wait_recv()
            halo_up.wait_send()

        @pl.when(tile < TILES - 1)
        def _():
            halo_up.wait_recv()
            halo_down.wait_send()

        for m in range(MB):
            for d, rs, r in ((0, -1, 0), (1, 1, ROWS - 1)):
                row = halo_r[d, m].astype(F32)
                for cs in (-1, 0, 1):
                    tap = 3 * (rs + 1) + cs + 1
                    taps[m, tap * C:(tap + 1) * C, r * L:(r + 1) * L] = rolled(row, -cs).astype(BF16)

    def forward(m, j):
        cols = pl.ds(pl.multiple_of(j * 256, 256), 256)
        v = dot(wt_v[...], taps[m, :, cols])
        v = v + jnp.concatenate([bcol[...]] * 2, axis=1)
        v2 = v * v
        t = jnp.tanh(v * (TANH_SCALE * CUBIC_TERM * v2 + TANH_SCALE))
        p = 0.5 * t + 0.5
        out = v * p
        hidden[m, :, cols] = out.astype(BF16)
        slope[m, :, cols] = p + out * (1.0 - p) * (6.0 * TANH_SCALE * CUBIC_TERM * v2 + 2.0 * TANH_SCALE)

    def total_row(m, r):
        return cot_v[m, pl.ds(r, C, stride=ROWS), :] + sg_r[m, r].astype(F32)

    def pre_grads(m):
        land = land_v[...].astype(F32)
        for r in range(ROWS):
            masked[m, :, r * L:(r + 1) * L] = (total_row(m, r) * land[r:r + 1, :]).astype(BF16)

        def step(j, carry):
            cols = pl.ds(pl.multiple_of(j * 256, 256), 256)
            grad = dot(wo_v[...], masked[m, :, cols]) * slope[m, :, cols]
            bias_acc[...] += grad[:, :L] + grad[:, L:]
            pre[m, :, pl.ds(pl.multiple_of(j * 256 + 256, 256), 256)] = grad.astype(BF16)
            return carry

        lax.fori_loop(0, ROWS // 2, step, 0)

    def weight_grads(m, first):
        p = pre[m, :, 256:256 + ROWS * L]
        for g in range(3):
            term = dot_t(taps[m, g * 384:(g + 1) * 384, :], p)

            @pl.when(first)
            def _():
                w1_acc[g * 384:(g + 1) * 384, :] = term

            @pl.when(jnp.logical_not(first))
            def _():
                w1_acc[g * 384:(g + 1) * 384, :] += term

        term = dot_t(hidden[m], masked[m])

        @pl.when(first)
        def _():
            w2_acc[...] = term

        @pl.when(jnp.logical_not(first))
        def _():
            w2_acc[...] += term

    def conv_back(m, k):
        acc = jnp.zeros((3 * C, 2 * L), F32)
        for rs in (-1, 0, 1):
            start = pl.multiple_of((2 * k + 1 - rs) * L, L)
            acc = acc + dot(w_v[(rs + 1) * 384:(rs + 2) * 384, :], pre[m, :, pl.ds(start, 2 * L)])
        rows = []
        for half in range(2):
            lanes = slice(half * L, (half + 1) * L)
            rows.append(rolled(acc[:C, lanes], -1) + acc[C:2 * C, lanes] + rolled(acc[2 * C:, lanes], 1))
        return rows

    def edges(m):
        up = remote(edge_s.at[m, 0], edge_r.at[m, 1], edge_ss.at[m, 0], edge_rs.at[m, 1], (lead, tile - 1))
        down = remote(edge_s.at[m, 1], edge_r.at[m, 0], edge_ss.at[m, 1], edge_rs.at[m, 0], (lead, tile + 1))
        return up, down

    def sg_copy(m, i):
        rows = pl.ds(1 + 2 * i, 2) if isinstance(i, int) and i < 3 else None
        if rows is None:
            rows = pl.ds(0 if i == 3 else ROWS - 1, 1)
        return remote(sg_s.at[m, rows], sg_r.at[m, rows], sg_ss.at[m, i], sg_rs.at[m, i], (1 - lead, tile))

    def finish_row(m, r, grad):
        value = total_row(m, r) + grad
        out_v[m, pl.ds(r, C, stride=ROWS), :] = value
        sg_s[m, r] = value.astype(BF16)

    def input_grads(m):
        up, down = edges(m)
        top, part[0] = conv_back(m, 0)
        edge_s[m, 0] = top

        @pl.when(tile > 0)
        def _():
            up.start()

        part[1], bottom = conv_back(m, ROWS // 2)
        edge_s[m, 1] = bottom

        @pl.when(tile < TILES - 1)
        def _():
            down.start()

        for k in range(1, ROWS // 2):
            for half, grad in enumerate(conv_back(m, k)):
                finish_row(m, 2 * k - 1 + half, grad)

            @pl.when(lead == 1)
            def _():
                sg_copy(m, k - 1).start()

        for d, r in ((0, 0), (1, ROWS - 1)):
            @pl.when(tile > 0 if d == 0 else tile < TILES - 1)
            def _():
                (down if d == 0 else up).wait_recv()
                (up if d == 0 else down).wait_send()
                finish_row(m, r, part[d] + edge_r[m, d])

            @pl.when(tile == 0 if d == 0 else tile == TILES - 1)
            def _():
                finish_row(m, r, part[d])

            @pl.when(lead == 1)
            def _():
                sg_copy(m, 3 + d).start()

        pltpu.make_async_copy(out_v.at[m], out_hbm.at[m], out_sem.at[m]).start()

    def piece(b, half):
        return (
            w1_acc[pl.ds(pl.multiple_of(b * 144, 8), 144), pl.ds(pl.multiple_of(half * 256, 256), 256)],
            jnp.concatenate(
                [w2_acc[pl.ds(pl.multiple_of(b * 64 + half * 32 + q * 16, 16), 16), :] for q in range(2)], axis=1
            ),
            jnp.broadcast_to(b_row[:, pl.ds(pl.multiple_of(half * 256, 256), 256)], (16, 256)),
        )

    pair = (lead, tile + 1 - 2 * core)

    def c_copy(k):
        b = lax.rem(block + 1 + k, BLOCKS)
        return b, remote(c_s.at[b], c_r.at[b], c_ss.at[k], c_rs.at[k], pair)

    def y_copy(k):
        b = lax.rem(block + 1 + k, BLOCKS)
        return b, remote(y_s.at[b], y_r.at[k], y_ss.at[k], y_rs.at[k], (lead, b * LOCAL + local))

    def start_core_stage():
        for j in range(4):
            b_row[:, j * 128:(j + 1) * 128] = jnp.sum(bias_acc[j * 128:(j + 1) * 128, :].T, axis=0, keepdims=True)

        def step(k, carry):
            b, copy = c_copy(k)
            one, two, three = piece(b, 1 - core)
            c_s[b, :144, :] = one.astype(BF16)
            c_s[b, 144:160, :] = two.astype(BF16)
            c_s[b, 160:, :] = three.astype(BF16)
            copy.start()
            return carry

        lax.fori_loop(0, BLOCKS, step, 0)

    def sweep(it, carry):
        m = lax.rem(it, MB)
        ahead = it < MB

        @pl.when(ahead)
        def _():
            @pl.when(it == 0)
            def _():
                forward(m, 1)
                forward(m, 2)
                halo_arrived()
                forward(m, 0)
                forward(m, 3)

            @pl.when(it == 1)
            def _():
                lax.fori_loop(0, 4, lambda j, c: (forward(m, j), c)[1], 0)

        mine = jnp.where(ahead, lead == 1, lead == 0)

        @pl.when(mine)
        def _():
            @pl.when(lead == 0)
            def _():
                for i in range(5):
                    sg_copy(m, i).wait_recv()

            pre_grads(m)

        @pl.when(jnp.logical_not(ahead))
        def _():
            weight_grads(m, it == MB)

        @pl.when(it == 2 * MB - 1)
        def _():
            start_core_stage()

        @pl.when(mine)
        def _():
            input_grads(m)

        return carry

    lax.fori_loop(0, 2 * MB, sweep, 0)

    def y_step(k, carry):
        b, copy = c_copy(k)
        copy.wait_recv()
        for value, lo, hi in zip(piece(b, core), (0, 144, 160), (144, 160, BROWS)):
            value = value + c_r[b, lo:hi, :].astype(F32)
            y_sum[lo:hi, :] = value
            y_s[b, lo:hi, :] = value.astype(BF16)

        @pl.when(k < BLOCKS - 1)
        def _():
            y_copy(k)[1].start()

        return carry

    lax.fori_loop(0, BLOCKS, y_step, 0)

    for k in range(BLOCKS - 1):
        y_copy(k)[1].wait_recv()
        y_sum[...] += y_r[k].astype(F32)

    def f_copy(k):
        to = lax.rem(local + k, LOCAL)
        return remote(f_s.at[to], f_r.at[local], f_ss.at[k], f_rs.at[k], (lead, block * LOCAL + to))

    def f_landed(k):
        source = lax.rem(local + LOCAL - k, LOCAL)
        return remote(f_s.at[local], f_r.at[source], f_ss.at[k], f_rs.at[k], (lead, block * LOCAL + source))

    row_id = lax.broadcasted_iota(jnp.int32, (24, 256), 0)
    for j in range(LOCAL):
        rows = y_sum[18 * j:18 * j + 24, :]
        bias = jnp.broadcast_to(y_sum[160:161, :], (24, 256))
        lead_rows = jnp.where(row_id < 18, rows, bias)
        q = (j // 2) % 2
        tail = y_sum[144 + 8 * (j % 2):152 + 8 * (j % 2), q * 128:(q + 1) * 128]
        tail = jnp.concatenate([tail, jnp.zeros_like(tail)], axis=1)
        f_s[j] = jnp.concatenate([lead_rows, tail], axis=0).astype(BF16)
    for k in range(1, LOCAL):
        f_copy(k).start()
    f_r[local] = f_s[local]
    for k in range(1, LOCAL):
        f_landed(k).wait_recv()

    for half in range(2):
        total = f_r[half].astype(F32)
        for x in range(1, 4):
            total = total + f_r[2 * x + half].astype(F32)
        l_s[:, half * 256:(half + 1) * 256] = total
    tail_core = lax.div(xpos, 2)
    total = f_r[tail_core, 16:32, :L].astype(F32)
    for x in range(1, 4):
        total = total + f_r[2 * x + tail_core, 16:32, :L].astype(F32)
    l_s[24:32, :L] = total[8:16]

    l_copy = remote(l_s, l_r, l_ss, l_rs, (1 - lead, tile))
    l_copy.start()
    l_copy.wait_recv()
    result = (l_s[...] + l_r[...]) * scale
    w1_out[...] = result[:18]
    w2_out[...] = result[24:32, :L]
    b1 = result[18:19, :L]
    for q in range(1, 4):
        b1 = jnp.where(lax.div(tile, 16) == q, result[18:19, q * L:(q + 1) * L], b1)
    b1_out[...] = pltpu.roll(b1, lax.rem(L - 8 * lax.rem(tile, 16), L), 1)

    @pl.when(lead == 1)
    def _():
        for m in range(MB):
            for i in range(5):
                sg_copy(m, i).wait_send()

    for k in range(BLOCKS):
        c_copy(k)[1].wait_send()
    for k in range(BLOCKS - 1):
        y_copy(k)[1].wait_send()
    for k in range(1, LOCAL):
        f_copy(k).wait_send()
    l_copy.wait_send()
    for m in range(MB):
        pltpu.make_async_copy(out_v.at[m], out_hbm.at[m], out_sem.at[m]).wait()


def shards(states, cotangents, w_conv, b_conv, w_out, forcing, land, dates):
    grad_scale = 1.0 / math.sqrt(2 * MB * TILES * ROWS * L)
    any_spec = pl.BlockSpec(memory_space=pl.ANY)
    vmem_spec = pl.BlockSpec(memory_space=pltpu.VMEM)
    dma = pltpu.SemaphoreType.DMA
    flat = (MB, C * ROWS, L)
    out, w1, w2, b1 = pl.pallas_call(
        functools.partial(kernel, grad_scale),
        out_shape=(
            jax.ShapeDtypeStruct(flat, F32),
            jax.ShapeDtypeStruct((18, H), F32),
            jax.ShapeDtypeStruct((8, C), F32),
            jax.ShapeDtypeStruct((1, L), F32),
        ),
        in_specs=[pl.BlockSpec(memory_space=pltpu.SMEM)] + [any_spec] * 7,
        out_specs=(any_spec, vmem_spec, vmem_spec, vmem_spec),
        scratch_shapes=[
            pltpu.VMEM(flat, F32),
            pltpu.VMEM(flat, F32),
            pltpu.VMEM((9 * C, H), BF16),
            pltpu.VMEM((H, 9 * C), BF16),
            pltpu.VMEM((1, H), F32),
            pltpu.VMEM((H, C), BF16),
            pltpu.VMEM(forcing.shape, F32),
            pltpu.VMEM((ROWS, L), jnp.int32),
            pltpu.VMEM((H, L), F32),
            pltpu.VMEM((MB, C, L), F32),
            pltpu.VMEM((MB, 9 * C, ROWS * L), BF16),
            pltpu.VMEM((2, MB, C, L), BF16),
            pltpu.VMEM((2, MB, C, L), BF16),
            pltpu.VMEM((MB, H, ROWS * L), BF16),
            pltpu.VMEM((MB, H, ROWS * L), F32),
            pltpu.VMEM((MB, C, ROWS * L), BF16),
            pltpu.VMEM((MB, H, (ROWS + 4) * L), BF16),
            pltpu.VMEM((H, L), F32),
            pltpu.VMEM((MB, 2, C, L), F32),
            pltpu.VMEM((MB, 2, C, L), F32),
            pltpu.VMEM((2, C, L), F32),
            pltpu.VMEM((MB, ROWS, C, L), BF16),
            pltpu.VMEM((MB, ROWS, C, L), BF16),
            pltpu.VMEM(flat, F32),
            pltpu.VMEM((9 * C, H), F32),
            pltpu.VMEM((H, C), F32),
            pltpu.VMEM((1, H), F32),
            pltpu.VMEM((BLOCKS, BROWS, 256), BF16),
            pltpu.VMEM((BLOCKS, BROWS, 256), BF16),
            pltpu.VMEM((BLOCKS, BROWS, 256), BF16),
            pltpu.VMEM((BLOCKS - 1, BROWS, 256), BF16),
            pltpu.VMEM((BROWS, 256), F32),
            pltpu.VMEM((LOCAL, 32, 256), BF16),
            pltpu.VMEM((LOCAL, 32, 256), BF16),
            pltpu.VMEM((32, H), F32),
            pltpu.VMEM((32, H), F32),
            dma((7,)), dma((MB,)), dma((2,)), dma((2,)), dma((MB, 2)), dma((MB, 2)), dma((MB, 5)), dma((MB, 5)),
            dma((BLOCKS,)), dma((BLOCKS,)), dma((BLOCKS - 1,)), dma((BLOCKS - 1,)), dma((LOCAL,)), dma((LOCAL,)), dma, dma,
        ],
        compiler_params=pltpu.CompilerParams(collective_id=0, has_side_effects=True, vmem_limit_bytes=56 << 20),
    )(
        dates,
        states.reshape(flat),
        cotangents.reshape(flat),
        w_conv,
        b_conv.reshape(1, H),
        w_out,
        forcing,
        land,
    )
    return out.reshape(states.shape), w1, w2, b1[0, :8]


def solution(mesh):
    placed = (
        P("lead", None, None, "tile", None),
        P("lead", None, None, "tile", None),
        P(),
        P(),
        P(),
        P(),
        P("tile", None),
        P(),
    )
    return jax.shard_map(
        shards,
        mesh=mesh,
        in_specs=placed,
        out_specs=(
            P("lead", None, None, "tile", None),
            P("tile", None),
            P("tile", None),
            P("tile"),
        ),
        check_vma=False,
    )
```

```python
import functools
import math

import jax
import jax.numpy as jnp
from jax import lax
from jax.experimental import pallas as pl
from jax.experimental.pallas import tpu as pltpu
from jax.sharding import PartitionSpec as P

MESH = pl.DeviceIdType.MESH
TANH_SCALE = 0.7978845608028654
CUBIC_TERM = 0.044715
F32 = jnp.float32
BF16 = jnp.bfloat16

C = 128
H = 512
ROWS = 8
L = 128
MB = 2
TILES = 64
BLOCKS = 8
LOCAL = 8
BROWS = 176


def remote(src, dst, send_sem, recv_sem, device):
    return pltpu.make_async_remote_copy(
        src_ref=src, dst_ref=dst, send_sem=send_sem, recv_sem=recv_sem,
        device_id=device, device_id_type=MESH,
    )


def dot(a, b):
    return jnp.dot(a, b, preferred_element_type=F32)


def dot_t(a, b):
    return lax.dot_general(a, b, (((1,), (1,)), ((), ())), preferred_element_type=F32)


def rolled(value, shift):
    return value if shift % L == 0 else pltpu.roll(value, shift % L, 1)


def kernel(
    scale,
    dates, x_hbm, cot_hbm, w_hbm, b_hbm, wo_hbm, f_hbm, land_hbm,
    out_v, w1_out, w2_out, b1_out,
    x_v, cot_v, w_v, wt_v, w_cat, w_edge, b_v, wo_v, f_v, land_v,
    bcol, shift, taps, halo_s, halo_r, hidden, slope, masked, pre, bias_acc,
    edge_s, edge_r, part, sg_s, sg_r, w1_acc, w2_acc, b_row,
    c_s, c_r, y_s, y_r, y_sum, f_t, f_s, f_r, l_s, l_r,
    in_sem, halo_ss, halo_rs, edge_ss, edge_rs, sg_ss, sg_rs,
    c_ss, c_rs, y_ss, y_rs, f_ss, f_rs, l_ss, l_rs,
):
    lead = lax.axis_index("lead")
    tile = lax.axis_index("tile")
    core = lax.rem(tile, 2)
    local = lax.rem(tile, LOCAL)
    block = lax.div(tile, LOCAL)
    xpos = lax.div(local, 2)

    peers = [(lead, lax.rem(tile + 1, TILES)), (lead, lax.rem(tile + TILES - 1, TILES)), (1 - lead, tile)]
    peers += [(lead, lax.rem(block + k, BLOCKS) * LOCAL + local) for k in range(1, BLOCKS)]
    peers += [(which, block * LOCAL + lax.rem(local + k, LOCAL)) for k in range(1, LOCAL) for which in (lead, 1 - lead)]
    barrier = pltpu.get_barrier_semaphore()
    for peer in peers:
        pl.semaphore_signal(barrier, inc=1, device_id=peer, device_id_type=MESH)

    loads = [
        pltpu.make_async_copy(src, dst, in_sem.at[i])
        for i, (src, dst) in enumerate(
            [(f_hbm, f_v), (x_hbm, x_v), (w_hbm, w_v), (b_hbm, b_v), (cot_hbm, cot_v), (land_hbm, land_v), (wo_hbm, wo_v)]
        )
    ]
    for load in loads:
        load.start()

    loads[0].wait()
    for m in range(MB):
        day = lax.rem(dates[m] + lead, f_hbm.shape[0])
        shift[m] = jnp.broadcast_to(f_v[pl.ds(day, 1), :], (C, L)).T
    loads[1].wait()
    for m in range(MB):
        for d, r in ((0, 0), (1, ROWS - 1)):
            halo_s[d, m] = (x_v[m, pl.ds(r, C, stride=ROWS), :] + shift[m]).astype(BF16)
    for m in range(MB):
        for r in range(ROWS):
            rounded = (x_v[m, pl.ds(r, C, stride=ROWS), :] + shift[m])
            for cs in (-1, 0, 1):
                view = rolled(rounded, -cs).astype(BF16)
                for rs in (-1, 0, 1):
                    if 0 <= r - rs < ROWS:
                        tap = 3 * (rs + 1) + cs + 1
                        taps[m, tap * C:(tap + 1) * C, (r - rs) * L:(r - rs + 1) * L] = view

    loads[2].wait()
    for i in range(9):
        for j in range(4):
            wt_v[j * 128:(j + 1) * 128, i * 128:(i + 1) * 128] = w_v[i * 128:(i + 1) * 128, j * 128:(j + 1) * 128].T
    loads[3].wait()
    for j in range(4):
        bcol[j * 128:(j + 1) * 128, :] = jnp.broadcast_to(b_v[:, j * 128:(j + 1) * 128], (L, L)).T
    for rs in range(3):
        w_cat[:, rs * H:(rs + 1) * H] = w_v[rs * 384:(rs + 1) * 384, :]
        if rs != 1:
            w_edge[rs // 2 * 384:(rs // 2 + 1) * 384, :] = w_v[rs * 384:(rs + 1) * 384, :]
    pl.semaphore_wait(barrier, len(peers))
    halo_up = remote(halo_s.at[0], halo_r.at[1], halo_ss.at[0], halo_rs.at[1], (lead, tile - 1))
    halo_down = remote(halo_s.at[1], halo_r.at[0], halo_ss.at[1], halo_rs.at[0], (lead, tile + 1))

    @pl.when(tile > 0)
    def _():
        halo_up.start()

    @pl.when(tile < TILES - 1)
    def _():
        halo_down.start()

    @pl.when(tile == 0)
    def _():
        halo_r[0] = jnp.zeros_like(halo_r[0])

    @pl.when(tile == TILES - 1)
    def _():
        halo_r[1] = jnp.zeros_like(halo_r[1])

    for lanes in (slice(0, L), slice((ROWS + 1) * L, (ROWS + 2) * L)):
        pre[:, :, lanes] = jnp.zeros((MB, H, L), BF16)
    bias_acc[...] = jnp.zeros_like(bias_acc)

    @pl.when(lead == 1)
    def _():
        sg_r[...] = jnp.zeros_like(sg_r)

    for load in loads[4:]:
        load.wait()

    def halo_arrived():
        @pl.when(tile > 0)
        def _():
            halo_down.wait_recv()
            halo_up.wait_send()

        @pl.when(tile < TILES - 1)
        def _():
            halo_up.wait_recv()
            halo_down.wait_send()

        for m in range(MB):
            for d, rs, r in ((0, -1, 0), (1, 1, ROWS - 1)):
                row = halo_r[d, m].astype(F32)
                for cs in (-1, 0, 1):
                    tap = 3 * (rs + 1) + cs + 1
                    taps[m, tap * C:(tap + 1) * C, r * L:(r + 1) * L] = rolled(row, -cs).astype(BF16)

    def forward(m, spans):
        for lo, hi in spans:
            cols = slice(lo * L, hi * L)
            v = dot(wt_v[...], taps[m, :, cols])
            v = v + jnp.concatenate([bcol[...]] * (hi - lo), axis=1)
            v2 = v * v
            t = jnp.tanh(v * (TANH_SCALE * CUBIC_TERM * v2 + TANH_SCALE))
            p = 0.5 * t + 0.5
            out = v * p
            hidden[m, :, cols] = out.astype(BF16)
            slope[m, :, cols] = p + out * (1.0 - p) * (6.0 * TANH_SCALE * CUBIC_TERM * v2 + 2.0 * TANH_SCALE)

    def total_row(m, r):
        return cot_v[m, pl.ds(r, C, stride=ROWS), :] + sg_r[m, r].astype(F32)

    def pre_grads(m):
        land = land_v[...].astype(F32)
        for r in range(ROWS):
            masked[m, :, r * L:(r + 1) * L] = (total_row(m, r) * land[r:r + 1, :]).astype(BF16)

        for j in range(2):
            cols = slice(j * 512, (j + 1) * 512)
            grad = dot(wo_v[...], masked[m, :, cols]) * slope[m, :, cols]
            bias_acc[...] += (grad[:, :L] + grad[:, L:2 * L]) + (grad[:, 2 * L:3 * L] + grad[:, 3 * L:])
            pre[m, :, L + j * 512:L + (j + 1) * 512] = grad.astype(BF16)

    def weight_grads(m, first):
        p = pre[m, :, L:(ROWS + 1) * L]
        for g in range(3):
            term = dot_t(taps[m, g * 384:(g + 1) * 384, :], p)

            @pl.when(first)
            def _():
                w1_acc[g * 384:(g + 1) * 384, :] = term

            @pl.when(jnp.logical_not(first))
            def _():
                w1_acc[g * 384:(g + 1) * 384, :] += term

        term = dot_t(hidden[m], masked[m])

        @pl.when(first)
        def _():
            w2_acc[...] = term

        @pl.when(jnp.logical_not(first))
        def _():
            w2_acc[...] += term

    def gather_steps(acc, lanes):
        return rolled(acc[:C, lanes], -1) + acc[C:2 * C, lanes] + rolled(acc[2 * C:, lanes], 1)

    def conv_edges(m):
        both = dot(w_edge[...], jnp.concatenate([pre[m, :, L:2 * L], pre[m, :, ROWS * L:(ROWS + 1) * L]], axis=1))
        return gather_steps(both[:384], slice(0, L)), gather_steps(both[384:], slice(L, 2 * L))

    def conv_back(m, half):
        starts = [(half * 4 + 1 - rs) * L for rs in (-1, 0, 1)]
        acc = dot(w_cat[...], jnp.concatenate([pre[m, :, s:s + 4 * L] for s in starts], axis=0))
        return [gather_steps(acc, slice(i * L, (i + 1) * L)) for i in range(4)]

    def edges(m):
        up = remote(edge_s.at[m, 0], edge_r.at[m, 1], edge_ss.at[m, 0], edge_rs.at[m, 1], (lead, tile - 1))
        down = remote(edge_s.at[m, 1], edge_r.at[m, 0], edge_ss.at[m, 1], edge_rs.at[m, 0], (lead, tile + 1))
        return up, down

    def sg_copy(m, i):
        rows = pl.ds(*((1, 3), (4, 3), (0, 1), (ROWS - 1, 1))[i])
        return remote(sg_s.at[m, rows], sg_r.at[m, rows], sg_ss.at[m, i], sg_rs.at[m, i], (1 - lead, tile))

    def finish_row(m, r, value):
        out_v[m, pl.ds(r, C, stride=ROWS), :] = value
        sg_s[m, r] = value.astype(BF16)

    def input_grads(m):
        up, down = edges(m)
        edge_s[m, 0], edge_s[m, 1] = conv_edges(m)

        @pl.when(tile > 0)
        def _():
            up.start()

        @pl.when(tile < TILES - 1)
        def _():
            down.start()

        for half in range(2):
            for i, grad in enumerate(conv_back(m, half)):
                r = half * 4 + i
                if r in (0, ROWS - 1):
                    part[m, half] = total_row(m, r) + grad
                else:
                    finish_row(m, r, total_row(m, r) + grad)

            @pl.when(lead == 1)
            def _():
                sg_copy(m, half).start()

    def finish_edges(m):
        up, down = edges(m)
        for d, r in ((0, 0), (1, ROWS - 1)):
            @pl.when(tile > 0 if d == 0 else tile < TILES - 1)
            def _():
                (down if d == 0 else up).wait_recv()
                (up if d == 0 else down).wait_send()
                finish_row(m, r, part[m, d] + edge_r[m, d])

            @pl.when(tile == 0 if d == 0 else tile == TILES - 1)
            def _():
                finish_row(m, r, part[m, d])

            @pl.when(lead == 1)
            def _():
                sg_copy(m, 2 + d).start()

    def piece(b, half):
        return (
            w1_acc[pl.ds(pl.multiple_of(b * 144, 8), 144), pl.ds(pl.multiple_of(half * 256, 256), 256)],
            jnp.concatenate(
                [w2_acc[pl.ds(pl.multiple_of(b * 64 + half * 32 + q * 16, 16), 16), :] for q in range(2)], axis=1
            ),
            jnp.broadcast_to(b_row[:, pl.ds(pl.multiple_of(half * 256, 256), 256)], (16, 256)),
        )

    pair = (lead, tile + 1 - 2 * core)

    def c_copy(k):
        b = lax.rem(block + 1 + k, BLOCKS)
        return b, remote(c_s.at[b], c_r.at[b], c_ss.at[k], c_rs.at[k], pair)

    def y_copy(k):
        b = lax.rem(block + 1 + k, BLOCKS)
        return b, remote(y_s.at[b], y_r.at[k], y_ss.at[k], y_rs.at[k], (lead, b * LOCAL + local))

    def start_core_stage():
        for j in range(4):
            b_row[:, j * 128:(j + 1) * 128] = jnp.sum(bias_acc[j * 128:(j + 1) * 128, :].T, axis=0, keepdims=True)

        def step(k, carry):
            b, copy = c_copy(k)
            one, two, three = piece(b, 1 - core)
            c_s[b, :144, :] = one.astype(BF16)
            c_s[b, 144:160, :] = two.astype(BF16)
            c_s[b, 160:, :] = three.astype(BF16)
            copy.start()
            return carry

        lax.fori_loop(0, BLOCKS, step, 0)

    def sweep(it, carry):
        m = lax.rem(it, MB)
        ahead = it < MB

        @pl.when(ahead)
        def _():
            forward(m, ((0, 2), (6, 8)))

        @pl.when(jnp.where(lead == 1, (it == 1) | (it == MB), it == MB + 1))
        def _():
            finish_edges(1 - m)

        mine = jnp.where(ahead, lead == 1, lead == 0)

        @pl.when(mine)
        def _():
            @pl.when(lead == 0)
            def _():
                for i in range(4):
                    sg_copy(m, i).wait_recv()

            pre_grads(m)

        @pl.when(jnp.logical_not(ahead))
        def _():
            weight_grads(m, it == MB)

        @pl.when(it == 2 * MB - 1)
        def _():
            start_core_stage()

        @pl.when(mine)
        def _():
            input_grads(m)

        return carry

    forward(0, ((2, 6),))
    forward(1, ((2, 6),))
    halo_arrived()
    lax.fori_loop(0, 2 * MB, sweep, 0)

    def y_step(k, carry):
        b, copy = c_copy(k)
        copy.wait_recv()
        for value, lo, hi in zip(piece(b, core), (0, 144, 160), (144, 160, BROWS)):
            value = value + c_r[b, lo:hi, :].astype(F32)
            y_sum[lo:hi, :] = value
            y_s[b, lo:hi, :] = value.astype(BF16)

        @pl.when(k < BLOCKS - 1)
        def _():
            y_copy(k)[1].start()

        return carry

    lax.fori_loop(0, BLOCKS, y_step, 0)

    @pl.when(lead == 0)
    def _():
        finish_edges(MB - 1)

    for k in range(BLOCKS - 1):
        y_copy(k)[1].wait_recv()
        y_sum[...] += y_r[k].astype(F32)

    l_s[...] = y_sum[...].astype(BF16)
    l_copy = remote(l_s, l_r, l_ss, l_rs, (1 - lead, tile))

    @pl.when(lead == 1)
    def _():
        l_copy.start()

    def f_copy(k, which):
        to = lax.rem(local + k, LOCAL)
        return remote(
            f_s.at[to], f_r.at[local], f_ss.at[k, which], f_rs.at[k], (which, block * LOCAL + to)
        )

    def f_landed(k):
        source = lax.rem(local + LOCAL - k, LOCAL)
        return remote(f_s.at[local], f_r.at[source], f_ss.at[k, 0], f_rs.at[k], (1 - lead, tile))

    @pl.when(lead == 0)
    def _():
        l_copy.wait_recv()
        y_sum[...] += l_r[...].astype(F32)
        for j in range(LOCAL):
            f_t[j, :18, :] = y_sum[18 * j:18 * j + 18, :]
            f_t[j, 18:19, :] = y_sum[160:161, :]
            q = (j // 2) % 2
            for i in range(2):
                first = 144 + 8 * (j % 2) + 4 * i
                f_t[j, 19:23, i * L:(i + 1) * L] = y_sum[first:first + 4, q * L:(q + 1) * L]
            f_t[j, 23:24, :] = jnp.zeros((1, 256), F32)
            f_s[j] = f_t[j].astype(BF16)
        for k in range(LOCAL):
            f_copy(k, 1).start()
        for k in range(1, LOCAL):
            f_copy(k, 0).start()
        f_r[local] = f_s[local]

    @pl.when(lead == 1)
    def _():
        f_landed(0).wait_recv()

    for k in range(1, LOCAL):
        f_landed(k).wait_recv()

    for half in range(2):
        total = f_r[half].astype(F32)
        for x in range(1, 4):
            total = total + f_r[2 * x + half].astype(F32)
        total = total * scale
        w1_out[:, half * 256:(half + 1) * 256] = total[:18]
        b_row[:, half * 256:(half + 1) * 256] = total[18:19]
    tail_core = lax.div(xpos, 2)
    total = f_r[tail_core].astype(F32)
    for x in range(1, 4):
        total = total + f_r[2 * x + tail_core].astype(F32)
    total = total * scale
    w2_out[:4, :] = total[19:23, :L]
    w2_out[4:, :] = total[19:23, L:]
    b1 = b_row[:, :L]
    for q in range(1, 4):
        b1 = jnp.where(lax.div(tile, 16) == q, b_row[:, q * L:(q + 1) * L], b1)
    b1_out[...] = pltpu.roll(b1, lax.rem(L - 8 * lax.rem(tile, 16), L), 1)

    @pl.when(lead == 1)
    def _():
        for m in range(MB):
            for i in range(4):
                sg_copy(m, i).wait_send()
        l_copy.wait_send()

    @pl.when(lead == 0)
    def _():
        for k in range(LOCAL):
            f_copy(k, 1).wait_send()
        for k in range(1, LOCAL):
            f_copy(k, 0).wait_send()

    for k in range(BLOCKS):
        c_copy(k)[1].wait_send()
    for k in range(BLOCKS - 1):
        y_copy(k)[1].wait_send()


def deliver(*refs):
    held, outs, b1_own, sems = refs[:4], refs[4:8], refs[8], refs[9]
    b1_own[...] = held[3][0, :8]
    held = held[:3] + (b1_own,)
    copies = [pltpu.make_async_copy(src, dst, sems.at[i]) for i, (src, dst) in enumerate(zip(held, outs))]
    for copy in copies:
        copy.start()
    for copy in copies:
        copy.wait()


def shards(states, cotangents, w_conv, b_conv, w_out, forcing, land, dates):
    grad_scale = 1.0 / math.sqrt(2 * MB * TILES * ROWS * L)
    any_spec = pl.BlockSpec(memory_space=pl.ANY)
    vmem_spec = pl.BlockSpec(memory_space=pltpu.VMEM)
    dma = pltpu.SemaphoreType.DMA
    flat = (MB, C * ROWS, L)
    out, w1, w2, b1 = pl.pallas_call(
        functools.partial(kernel, grad_scale),
        out_shape=(
            pltpu.VMEM(flat, F32),
            pltpu.VMEM((18, H), F32),
            pltpu.VMEM((8, C), F32),
            pltpu.VMEM((1, L), F32),
        ),
        in_specs=[pl.BlockSpec(memory_space=pltpu.SMEM)] + [any_spec] * 7,
        out_specs=(vmem_spec, vmem_spec, vmem_spec, vmem_spec),
        scratch_shapes=[
            pltpu.VMEM(flat, F32),
            pltpu.VMEM(flat, F32),
            pltpu.VMEM((9 * C, H), BF16),
            pltpu.VMEM((H, 9 * C), BF16),
            pltpu.VMEM((3 * C, 3 * H), BF16),
            pltpu.VMEM((6 * C, H), BF16),
            pltpu.VMEM((1, H), F32),
            pltpu.VMEM((H, C), BF16),
            pltpu.VMEM(forcing.shape, F32),
            pltpu.VMEM((ROWS, L), jnp.int32),
            pltpu.VMEM((H, L), F32),
            pltpu.VMEM((MB, C, L), F32),
            pltpu.VMEM((MB, 9 * C, ROWS * L), BF16),
            pltpu.VMEM((2, MB, C, L), BF16),
            pltpu.VMEM((2, MB, C, L), BF16),
            pltpu.VMEM((MB, H, ROWS * L), BF16),
            pltpu.VMEM((MB, H, ROWS * L), F32),
            pltpu.VMEM((MB, C, ROWS * L), BF16),
            pltpu.VMEM((MB, H, (ROWS + 2) * L), BF16),
            pltpu.VMEM((H, L), F32),
            pltpu.VMEM((MB, 2, C, L), F32),
            pltpu.VMEM((MB, 2, C, L), F32),
            pltpu.VMEM((MB, 2, C, L), F32),
            pltpu.VMEM((MB, ROWS, C, L), BF16),
            pltpu.VMEM((MB, ROWS, C, L), BF16),
            pltpu.VMEM((9 * C, H), F32),
            pltpu.VMEM((H, C), F32),
            pltpu.VMEM((1, H), F32),
            pltpu.VMEM((BLOCKS, BROWS, 256), BF16),
            pltpu.VMEM((BLOCKS, BROWS, 256), BF16),
            pltpu.VMEM((BLOCKS, BROWS, 256), BF16),
            pltpu.VMEM((BLOCKS - 1, BROWS, 256), BF16),
            pltpu.VMEM((BROWS, 256), F32),
            pltpu.VMEM((LOCAL, 24, 256), F32),
            pltpu.VMEM((LOCAL, 24, 256), BF16),
            pltpu.VMEM((LOCAL, 24, 256), BF16),
            pltpu.VMEM((BROWS, 256), BF16),
            pltpu.VMEM((BROWS, 256), BF16),
            dma((7,)), dma((2,)), dma((2,)), dma((MB, 2)), dma((MB, 2)), dma((MB, 4)), dma((MB, 4)),
            dma((BLOCKS,)), dma((BLOCKS,)), dma((BLOCKS - 1,)), dma((BLOCKS - 1,)), dma((LOCAL, 2)), dma((LOCAL,)), dma, dma,
        ],
        compiler_params=pltpu.CompilerParams(collective_id=0, has_side_effects=True, vmem_limit_bytes=56 << 20),
    )(
        dates,
        states.reshape(flat),
        cotangents.reshape(flat),
        w_conv,
        b_conv.reshape(1, H),
        w_out,
        forcing,
        land,
    )
    out, w1, w2, b1 = pl.pallas_call(
        deliver,
        out_shape=(
            jax.ShapeDtypeStruct(flat, F32),
            jax.ShapeDtypeStruct((18, H), F32),
            jax.ShapeDtypeStruct((8, C), F32),
            jax.ShapeDtypeStruct((8,), F32),
        ),
        in_specs=[vmem_spec] * 4,
        out_specs=(any_spec,) * 4,
        scratch_shapes=[pltpu.VMEM((8,), F32), dma((4,))],
    )(*(pltpu.with_memory_space_constraint(value, pltpu.VMEM) for value in (out, w1, w2, b1)))
    return out.reshape(states.shape), w1, w2, b1


def solution(mesh):
    placed = (
        P("lead", None, None, "tile", None),
        P("lead", None, None, "tile", None),
        P(),
        P(),
        P(),
        P(),
        P("tile", None),
        P(),
    )
    return jax.shard_map(
        shards,
        mesh=mesh,
        in_specs=placed,
        out_specs=(
            P("lead", None, None, "tile", None),
            P("tile", None),
            P("tile", None),
            P("tile"),
        ),
        check_vma=False,
    )
```

```python
import functools
import math

import jax
import jax.numpy as jnp
from jax import lax
from jax.experimental import pallas as pl
from jax.experimental.pallas import tpu as pltpu
from jax.sharding import PartitionSpec as P

MESH = pl.DeviceIdType.MESH
TANH_SCALE = 0.7978845608028654
CUBIC_TERM = 0.044715
F32 = jnp.float32
BF16 = jnp.bfloat16

C = 128
H = 512
ROWS = 8
L = 128
MB = 2
TILES = 64
BLOCKS = 8
LOCAL = 8
BROWS = 168


def remote(src, dst, send_sem, recv_sem, device):
    return pltpu.make_async_remote_copy(
        src_ref=src, dst_ref=dst, send_sem=send_sem, recv_sem=recv_sem,
        device_id=device, device_id_type=MESH,
    )


def dot(a, b):
    return jnp.dot(a, b, preferred_element_type=F32)


def dot_t(a, b):
    return lax.dot_general(a, b, (((1,), (1,)), ((), ())), preferred_element_type=F32)


def rolled(value, shift):
    return value if shift % L == 0 else pltpu.roll(value, shift % L, 1)


def kernel(
    scale,
    dates, x_hbm, cot_hbm, w_hbm, b_hbm, wo_hbm, f_hbm, land_hbm,
    out_v, w1_out, w2_out, b1_out,
    x_v, cot_v, w_v, wt_v, w_cat, w_edge, b_v, wo_v, f_v, land_v,
    bcol, shift, taps, halo_s, halo_r, hidden, slope, masked, pre, bias_acc,
    edge_s, edge_r, part, sg_s, sg_r, w1_acc, w2_acc, b_row,
    c_s, c_r, y_s, y_r, y_sum, f_t, f_s, f_r, l_s, l_r,
    in_sem, halo_ss, halo_rs, edge_ss, edge_rs, sg_ss, sg_rs,
    c_ss, c_rs, y_ss, y_rs, f_ss, f_rs, l_ss, l_rs,
):
    lead = lax.axis_index("lead")
    tile = lax.axis_index("tile")
    core = lax.rem(tile, 2)
    local = lax.rem(tile, LOCAL)
    block = lax.div(tile, LOCAL)
    xpos = lax.div(local, 2)

    peers = [(lead, lax.rem(tile + 1, TILES)), (lead, lax.rem(tile + TILES - 1, TILES)), (1 - lead, tile)]
    peers += [(lead, lax.rem(block + k, BLOCKS) * LOCAL + local) for k in range(1, BLOCKS)]
    peers += [(which, block * LOCAL + lax.rem(local + k, LOCAL)) for k in range(1, LOCAL) for which in (lead, 1 - lead)]
    barrier = pltpu.get_barrier_semaphore()
    for peer in peers:
        pl.semaphore_signal(barrier, inc=1, device_id=peer, device_id_type=MESH)

    loads = [
        pltpu.make_async_copy(src, dst, in_sem.at[i])
        for i, (src, dst) in enumerate(
            [(f_hbm, f_v), (x_hbm, x_v), (w_hbm, w_v), (b_hbm, b_v), (cot_hbm, cot_v), (land_hbm, land_v), (wo_hbm, wo_v)]
        )
    ]
    for load in loads:
        load.start()

    loads[0].wait()
    for m in range(MB):
        day = lax.rem(dates[m] + lead, f_hbm.shape[0])
        shift[m] = jnp.broadcast_to(f_v[pl.ds(day, 1), :], (C, L)).T
    loads[1].wait()
    for m in range(MB):
        for d, r in ((0, 0), (1, ROWS - 1)):
            halo_s[d, m] = (x_v[m, pl.ds(r, C, stride=ROWS), :] + shift[m]).astype(BF16)
    for m in range(MB):
        for r in range(ROWS):
            rounded = (x_v[m, pl.ds(r, C, stride=ROWS), :] + shift[m])
            for cs in (-1, 0, 1):
                view = rolled(rounded, -cs).astype(BF16)
                for rs in (-1, 0, 1):
                    if 0 <= r - rs < ROWS:
                        tap = 3 * (rs + 1) + cs + 1
                        taps[m, tap * C:(tap + 1) * C, (r - rs) * L:(r - rs + 1) * L] = view

    loads[2].wait()
    for i in range(9):
        for j in range(4):
            wt_v[j * 128:(j + 1) * 128, i * 128:(i + 1) * 128] = w_v[i * 128:(i + 1) * 128, j * 128:(j + 1) * 128].T
    loads[3].wait()
    for j in range(4):
        bcol[j * 128:(j + 1) * 128, :] = jnp.broadcast_to(b_v[:, j * 128:(j + 1) * 128], (L, L)).T
    for rs in range(3):
        w_cat[:, rs * H:(rs + 1) * H] = w_v[rs * 384:(rs + 1) * 384, :]
        if rs != 1:
            w_edge[rs // 2 * 384:(rs // 2 + 1) * 384, :] = w_v[rs * 384:(rs + 1) * 384, :]
    pl.semaphore_wait(barrier, len(peers))
    above, below = (lead, lax.rem(tile + TILES - 1, TILES)), (lead, lax.rem(tile + 1, TILES))
    inside = (tile > 0, tile < TILES - 1)
    halo_up = remote(halo_s.at[0], halo_r.at[1], halo_ss.at[0], halo_rs.at[1], above)
    halo_down = remote(halo_s.at[1], halo_r.at[0], halo_ss.at[1], halo_rs.at[0], below)
    halo_up.start()
    halo_down.start()

    for lanes in (slice(0, L), slice((ROWS + 1) * L, (ROWS + 2) * L)):
        pre[:, :, lanes] = jnp.zeros((MB, H, L), BF16)
    bias_acc[...] = jnp.zeros_like(bias_acc)

    @pl.when(lead == 1)
    def _():
        sg_r[...] = jnp.zeros_like(sg_r)

    for load in loads[4:]:
        load.wait()

    def halo_arrived():
        halo_up.wait()
        halo_down.wait()
        for m in range(MB):
            for d, rs, r in ((0, -1, 0), (1, 1, ROWS - 1)):
                row = jnp.where(inside[d], halo_r[d, m].astype(F32), 0.0)
                for cs in (-1, 0, 1):
                    tap = 3 * (rs + 1) + cs + 1
                    taps[m, tap * C:(tap + 1) * C, r * L:(r + 1) * L] = rolled(row, -cs).astype(BF16)

    def forward(m, spans):
        for lo, hi in spans:
            cols = slice(lo * L, hi * L)
            v = dot(wt_v[...], taps[m, :, cols])
            v = v + jnp.concatenate([bcol[...]] * (hi - lo), axis=1)
            v2 = v * v
            t = jnp.tanh(v * (TANH_SCALE * CUBIC_TERM * v2 + TANH_SCALE))
            p = 0.5 * t + 0.5
            out = v * p
            hidden[m, :, cols] = out.astype(BF16)
            slope[m, :, cols] = p + out * (1.0 - p) * (6.0 * TANH_SCALE * CUBIC_TERM * v2 + 2.0 * TANH_SCALE)

    def total_row(m, r):
        return cot_v[m, pl.ds(r, C, stride=ROWS), :] + sg_r[m, r].astype(F32)

    def pre_grads(m, spans):
        land = land_v[...].astype(F32)
        for lo, hi in spans:
            for r in range(lo, hi):
                masked[m, :, r * L:(r + 1) * L] = (total_row(m, r) * land[r:r + 1, :]).astype(BF16)
            cols = slice(lo * L, hi * L)
            grad = dot(wo_v[...], masked[m, :, cols]) * slope[m, :, cols]
            sums = [grad[:, i * L:(i + 1) * L] for i in range(hi - lo)]
            while len(sums) > 1:
                sums = [a + b for a, b in zip(sums[::2], sums[1::2])] + sums[len(sums) // 2 * 2:]
            bias_acc[...] += sums[0]
            pre[m, :, (lo + 1) * L:(hi + 1) * L] = grad.astype(BF16)

    def columns(ref, members, rows, spans, offset):
        parts = [ref[m, rows, (lo + offset) * L:(hi + offset) * L] for m in members for lo, hi in spans]
        return parts[0] if len(parts) == 1 else jnp.concatenate(parts, axis=1)

    def weight_grads(members, spans, first):
        p = columns(pre, members, slice(None), spans, 1)
        for g in range(3):
            rows = slice(g * 384, (g + 1) * 384)
            term = dot_t(columns(taps, members, rows, spans, 0), p)
            w1_acc[rows, :] = term if first else w1_acc[rows, :] + term
        term = dot_t(columns(hidden, members, slice(None), spans, 0), columns(masked, members, slice(None), spans, 0))
        w2_acc[...] = term if first else w2_acc[...] + term

    def gather_steps(acc, lanes):
        return rolled(acc[:C, lanes], -1) + acc[C:2 * C, lanes] + rolled(acc[2 * C:, lanes], 1)

    def conv_edges(m):
        both = dot(w_edge[...], jnp.concatenate([pre[m, :, L:2 * L], pre[m, :, ROWS * L:(ROWS + 1) * L]], axis=1))
        return gather_steps(both[:384], slice(0, L)), gather_steps(both[384:], slice(L, 2 * L))

    def conv_back(m, spans):
        sides = [columns(pre, (m,), slice(None), spans, 1 - rs) for rs in (-1, 0, 1)]
        acc = dot(w_cat[...], jnp.concatenate(sides, axis=0))
        rows = [r for lo, hi in spans for r in range(lo, hi)]
        return [(r, gather_steps(acc, slice(i * L, (i + 1) * L))) for i, r in enumerate(rows)]

    def edges(m):
        up = remote(edge_s.at[m, 0], edge_r.at[m, 1], edge_ss.at[m, 0], edge_rs.at[m, 1], above)
        down = remote(edge_s.at[m, 1], edge_r.at[m, 0], edge_ss.at[m, 1], edge_rs.at[m, 0], below)
        return up, down

    def sg_copy(m, i):
        rows = pl.ds(*((3, 2), (1, 2), (5, 2), (0, 1), (ROWS - 1, 1))[i])
        return remote(sg_s.at[m, rows], sg_r.at[m, rows], sg_ss.at[m, i], sg_rs.at[m, i], (1 - lead, tile))

    def finish_row(m, r, value):
        out_v[m, pl.ds(r, C, stride=ROWS), :] = value
        sg_s[m, r] = value.astype(BF16)

    def send_edges(m):
        edge_s[m, 0], edge_s[m, 1] = conv_edges(m)
        for copy in edges(m):
            copy.start()

    def input_grads(m, spans):
        for r, grad in conv_back(m, spans):
            if r in (0, ROWS - 1):
                part[m, r // (ROWS - 1)] = total_row(m, r) + grad
            else:
                finish_row(m, r, total_row(m, r) + grad)

    def finish_edges(m):
        for copy in edges(m):
            copy.wait()
        for d, r in ((0, 0), (1, ROWS - 1)):
            finish_row(m, r, part[m, d] + jnp.where(inside[d], edge_r[m, d], 0.0))

    def piece(b, half):
        return (
            w1_acc[pl.ds(pl.multiple_of(b * 144, 8), 144), pl.ds(pl.multiple_of(half * 256, 256), 256)],
            jnp.concatenate(
                [w2_acc[pl.ds(pl.multiple_of(b * 64 + half * 32 + q * 16, 16), 16), :] for q in range(2)], axis=1
            ),
            jnp.broadcast_to(b_row[:, pl.ds(pl.multiple_of(half * 256, 256), 256)], (8, 256)),
        )

    pair = (lead, tile + 1 - 2 * core)

    def c_copy(k):
        b = lax.rem(block + 1 + k, BLOCKS)
        return b, remote(c_s.at[b], c_r.at[b], c_ss.at[k], c_rs.at[k], pair)

    def y_copy(k):
        b = lax.rem(block + 1 + k, BLOCKS)
        return b, remote(y_s.at[b], y_r.at[k], y_ss.at[k], y_rs.at[k], (lead, b * LOCAL + local))

    def start_core_stage():
        for j in range(4):
            b_row[:, j * 128:(j + 1) * 128] = jnp.sum(bias_acc[j * 128:(j + 1) * 128, :].T, axis=0, keepdims=True)

        for k in range(BLOCKS):
            b, copy = c_copy(k)
            one, two, three = piece(b, 1 - core)
            c_s[b, :144, :] = one.astype(BF16)
            c_s[b, 144:160, :] = two.astype(BF16)
            c_s[b, 160:, :] = three.astype(BF16)
            copy.start()

    inner, outer, whole = ((2, 6),), ((0, 2), (6, 8)), ((0, 4), (4, 8))
    most, ends = ((1, 7),), ((0, 1), (7, 8))

    @pl.when(lead == 1)
    def _():
        for m in range(MB):
            forward(m, inner)
            pre_grads(m, inner)
            input_grads(m, ((3, 5),))
            sg_copy(m, 0).start()
        halo_arrived()
        for m in range(MB):
            forward(m, outer)
            pre_grads(m, outer)
            input_grads(m, ((1, 3), (5, 7)))
            for i in (1, 2):
                sg_copy(m, i).start()
            send_edges(m)
        for m in range(MB):
            input_grads(m, ends)
        for m in range(MB):
            finish_edges(m)
            for i in (3, 4):
                sg_copy(m, i).start()
        for m in range(MB):
            weight_grads((m,), ((0, 8),), m == 0)

    @pl.when(lead == 0)
    def _():
        for m in range(MB):
            forward(m, inner)
        halo_arrived()
        for m in range(MB):
            forward(m, outer)
        for m in range(MB):
            for i in range(3):
                sg_copy(m, i).wait_recv()
            pre_grads(m, most)
            weight_grads((m,), most, m == 0)
        for m in range(MB):
            for i in (3, 4):
                sg_copy(m, i).wait_recv()
            pre_grads(m, ends)
        weight_grads((0, 1), ends, False)

    start_core_stage()

    @pl.when(lead == 0)
    def _():
        for m in range(MB):
            send_edges(m)

    for k in range(BLOCKS):
        b, copy = c_copy(k)
        copy.wait_recv()
        for value, lo, hi in zip(piece(b, core), (0, 144, 160), (144, 160, BROWS)):
            value = value + c_r[b, lo:hi, :].astype(F32)
            if k < BLOCKS - 1:
                y_s[b, lo:hi, :] = value.astype(BF16)
            else:
                y_sum[lo:hi, :] = value
        if k < BLOCKS - 1:
            y_copy(k)[1].start()

    @pl.when(lead == 0)
    def _():
        for m in range(MB):
            for span in whole:
                input_grads(m, (span,))
        for m in range(MB):
            finish_edges(m)

    for k in range(BLOCKS - 1):
        y_copy(k)[1].wait_recv()
        y_sum[...] += y_r[k].astype(F32)

    l_s[...] = y_sum[...].astype(BF16)
    l_copy = remote(l_s, l_r, l_ss, l_rs, (1 - lead, tile))

    @pl.when(lead == 1)
    def _():
        l_copy.start()

    def f_copy(k, which):
        to = lax.rem(local + k, LOCAL)
        return remote(
            f_s.at[to], f_r.at[local], f_ss.at[k, which], f_rs.at[k], (which, block * LOCAL + to)
        )

    def f_landed(k):
        source = lax.rem(local + LOCAL - k, LOCAL)
        return remote(f_s.at[local], f_r.at[source], f_ss.at[k, 0], f_rs.at[k], (1 - lead, tile))

    @pl.when(lead == 0)
    def _():
        l_copy.wait_recv()
        y_sum[...] += l_r[...].astype(F32)
        for j in range(LOCAL):
            f_t[j, :18, :] = y_sum[18 * j:18 * j + 18, :]
            f_t[j, 18:19, :] = y_sum[160:161, :]
            q = (j // 2) % 2
            for i in range(2):
                first = 144 + 8 * (j % 2) + 4 * i
                f_t[j, 19:23, i * L:(i + 1) * L] = y_sum[first:first + 4, q * L:(q + 1) * L]
            f_t[j, 23:24, :] = jnp.zeros((1, 256), F32)
            f_s[j] = f_t[j].astype(BF16)
        for k in range(LOCAL):
            f_copy(k, 1).start()
        for k in range(1, LOCAL):
            f_copy(k, 0).start()
        f_r[local] = f_s[local]

    @pl.when(lead == 1)
    def _():
        f_landed(0).wait_recv()

    for k in range(1, LOCAL):
        f_landed(k).wait_recv()

    for half in range(2):
        total = f_r[half].astype(F32)
        for x in range(1, 4):
            total = total + f_r[2 * x + half].astype(F32)
        total = total * scale
        w1_out[:, half * 256:(half + 1) * 256] = total[:18]
        b_row[:, half * 256:(half + 1) * 256] = total[18:19]
    tail_core = lax.div(xpos, 2)
    total = f_r[tail_core].astype(F32)
    for x in range(1, 4):
        total = total + f_r[2 * x + tail_core].astype(F32)
    total = total * scale
    w2_out[:4, :] = total[19:23, :L]
    w2_out[4:, :] = total[19:23, L:]
    b1 = b_row[:, :L]
    for q in range(1, 4):
        b1 = jnp.where(lax.div(tile, 16) == q, b_row[:, q * L:(q + 1) * L], b1)
    b1_out[...] = pltpu.roll(b1, lax.rem(L - 8 * lax.rem(tile, 16), L), 1)

    @pl.when(lead == 1)
    def _():
        for m in range(MB):
            for i in range(5):
                sg_copy(m, i).wait_send()
        l_copy.wait_send()

    @pl.when(lead == 0)
    def _():
        for k in range(LOCAL):
            f_copy(k, 1).wait_send()
        for k in range(1, LOCAL):
            f_copy(k, 0).wait_send()

    for k in range(BLOCKS):
        c_copy(k)[1].wait_send()
    for k in range(BLOCKS - 1):
        y_copy(k)[1].wait_send()


def deliver(*refs):
    held, outs, b1_own, sems = refs[:4], refs[4:8], refs[8], refs[9]
    b1_own[...] = held[3][0, :8]
    held = held[:3] + (b1_own,)
    copies = [pltpu.make_async_copy(src, dst, sems.at[i]) for i, (src, dst) in enumerate(zip(held, outs))]
    for copy in copies:
        copy.start()
    for copy in copies:
        copy.wait()


def shards(states, cotangents, w_conv, b_conv, w_out, forcing, land, dates):
    grad_scale = 1.0 / math.sqrt(2 * MB * TILES * ROWS * L)
    any_spec = pl.BlockSpec(memory_space=pl.ANY)
    vmem_spec = pl.BlockSpec(memory_space=pltpu.VMEM)
    dma = pltpu.SemaphoreType.DMA
    flat = (MB, C * ROWS, L)
    out, w1, w2, b1 = pl.pallas_call(
        functools.partial(kernel, grad_scale),
        out_shape=(
            pltpu.VMEM(flat, F32),
            pltpu.VMEM((18, H), F32),
            pltpu.VMEM((8, C), F32),
            pltpu.VMEM((1, L), F32),
        ),
        in_specs=[pl.BlockSpec(memory_space=pltpu.SMEM)] + [any_spec] * 7,
        out_specs=(vmem_spec, vmem_spec, vmem_spec, vmem_spec),
        scratch_shapes=[
            pltpu.VMEM(flat, F32),
            pltpu.VMEM(flat, F32),
            pltpu.VMEM((9 * C, H), BF16),
            pltpu.VMEM((H, 9 * C), BF16),
            pltpu.VMEM((3 * C, 3 * H), BF16),
            pltpu.VMEM((6 * C, H), BF16),
            pltpu.VMEM((1, H), F32),
            pltpu.VMEM((H, C), BF16),
            pltpu.VMEM(forcing.shape, F32),
            pltpu.VMEM((ROWS, L), jnp.int32),
            pltpu.VMEM((H, L), F32),
            pltpu.VMEM((MB, C, L), F32),
            pltpu.VMEM((MB, 9 * C, ROWS * L), BF16),
            pltpu.VMEM((2, MB, C, L), BF16),
            pltpu.VMEM((2, MB, C, L), BF16),
            pltpu.VMEM((MB, H, ROWS * L), BF16),
            pltpu.VMEM((MB, H, ROWS * L), F32),
            pltpu.VMEM((MB, C, ROWS * L), BF16),
            pltpu.VMEM((MB, H, (ROWS + 2) * L), BF16),
            pltpu.VMEM((H, L), F32),
            pltpu.VMEM((MB, 2, C, L), F32),
            pltpu.VMEM((MB, 2, C, L), F32),
            pltpu.VMEM((MB, 2, C, L), F32),
            pltpu.VMEM((MB, ROWS, C, L), BF16),
            pltpu.VMEM((MB, ROWS, C, L), BF16),
            pltpu.VMEM((9 * C, H), F32),
            pltpu.VMEM((H, C), F32),
            pltpu.VMEM((1, H), F32),
            pltpu.VMEM((BLOCKS, BROWS, 256), BF16),
            pltpu.VMEM((BLOCKS, BROWS, 256), BF16),
            pltpu.VMEM((BLOCKS, BROWS, 256), BF16),
            pltpu.VMEM((BLOCKS - 1, BROWS, 256), BF16),
            pltpu.VMEM((BROWS, 256), F32),
            pltpu.VMEM((LOCAL, 24, 256), F32),
            pltpu.VMEM((LOCAL, 24, 256), BF16),
            pltpu.VMEM((LOCAL, 24, 256), BF16),
            pltpu.VMEM((BROWS, 256), BF16),
            pltpu.VMEM((BROWS, 256), BF16),
            dma((7,)), dma((2,)), dma((2,)), dma((MB, 2)), dma((MB, 2)), dma((MB, 5)), dma((MB, 5)),
            dma((BLOCKS,)), dma((BLOCKS,)), dma((BLOCKS - 1,)), dma((BLOCKS - 1,)), dma((LOCAL, 2)), dma((LOCAL,)), dma, dma,
        ],
        compiler_params=pltpu.CompilerParams(collective_id=0, has_side_effects=True, vmem_limit_bytes=56 << 20),
    )(
        dates,
        states.reshape(flat),
        cotangents.reshape(flat),
        w_conv,
        b_conv.reshape(1, H),
        w_out,
        forcing,
        land,
    )
    out, w1, w2, b1 = pl.pallas_call(
        deliver,
        out_shape=(
            jax.ShapeDtypeStruct(flat, F32),
            jax.ShapeDtypeStruct((18, H), F32),
            jax.ShapeDtypeStruct((8, C), F32),
            jax.ShapeDtypeStruct((8,), F32),
        ),
        in_specs=[vmem_spec] * 4,
        out_specs=(any_spec,) * 4,
        scratch_shapes=[pltpu.VMEM((8,), F32), dma((4,))],
    )(*(pltpu.with_memory_space_constraint(value, pltpu.VMEM) for value in (out, w1, w2, b1)))
    return out.reshape(states.shape), w1, w2, b1


def solution(mesh):
    placed = (
        P("lead", None, None, "tile", None),
        P("lead", None, None, "tile", None),
        P(),
        P(),
        P(),
        P(),
        P("tile", None),
        P(),
    )
    return jax.shard_map(
        shards,
        mesh=mesh,
        in_specs=placed,
        out_specs=(
            P("lead", None, None, "tile", None),
            P("tile", None),
            P("tile", None),
            P("tile"),
        ),
        check_vma=False,
    )
```

```python
import functools
import math

import jax
import jax.numpy as jnp
from jax import lax
from jax.experimental import pallas as pl
from jax.experimental.pallas import tpu as pltpu
from jax.sharding import PartitionSpec as P

MESH = pl.DeviceIdType.MESH
TANH_SCALE = 0.7978845608028654
CUBIC_TERM = 0.044715
F32 = jnp.float32
BF16 = jnp.bfloat16

C = 128
H = 512
ROWS = 8
L = 128
MB = 2
TILES = 64
BLOCKS = 8
LOCAL = 8
BROWS = 184
XROWS = 40


def remote(src, dst, send_sem, recv_sem, device):
    return pltpu.make_async_remote_copy(
        src_ref=src, dst_ref=dst, send_sem=send_sem, recv_sem=recv_sem,
        device_id=device, device_id_type=MESH,
    )


def dot(a, b):
    return jnp.dot(a, b, preferred_element_type=F32)


def dot_t(a, b):
    return lax.dot_general(a, b, (((1,), (1,)), ((), ())), preferred_element_type=F32)


def aligned(index, size):
    return index if isinstance(index, int) else pl.multiple_of(index, size)


def rolled(value, shift):
    return value if shift % L == 0 else pltpu.roll(value, shift % L, 1)


def kernel(
    scale,
    dates, x_hbm, cot_hbm, w_hbm, b_hbm, wo_hbm, f_hbm, land_hbm,
    out_v, w1_out, w2_out, b1_out,
    x_v, cot_v, w_v, wt_v, w_cat, w_edge, b_v, wo_v, f_v, land_v,
    bcol, shift, taps, halo_s, halo_r, hidden, slope, masked, pre, bias_acc,
    edge_s, edge_r, part, sg_s, sg_r, w1_acc, w2_acc, b_row,
    c_s, c_r, y_s, y_r, y_sum, f_t, f_s, f_r, l0_s, l0_r, x_s, x_r, x_t, g_s, g_r, l1_s, l1_r,
    in_sem, halo_ss, halo_rs, edge_ss, edge_rs, sg_ss, sg_rs,
    c_ss, c_rs, y_ss, y_rs, f_ss, f_rs, x_ss, x_rs, g_ss, g_rs, l_ss, l_rs,
):
    lead = lax.axis_index("lead")
    tile = lax.axis_index("tile")
    core = lax.rem(tile, 2)
    local = lax.rem(tile, LOCAL)
    block = lax.div(tile, LOCAL)
    xpos = lax.div(local, 2)

    loads = [
        pltpu.make_async_copy(src, dst, in_sem.at[i])
        for i, (src, dst) in enumerate(
            [(f_hbm, f_v), (x_hbm, x_v), (w_hbm, w_v), (b_hbm, b_v), (cot_hbm, cot_v), (land_hbm, land_v), (wo_hbm, wo_v)]
        )
    ]
    for load in loads:
        load.start()

    peers = [(lead, lax.rem(tile + 1, TILES)), (lead, lax.rem(tile + TILES - 1, TILES)), (1 - lead, tile)]
    others = [lax.rem(block + k, BLOCKS) * LOCAL + 2 * xpos + c for k in range(1, BLOCKS) for c in range(2)]
    others += [block * LOCAL + lax.rem(local + k, LOCAL) for k in range(1, LOCAL)]
    peers += [(which, other) for other in others for which in (lead, 1 - lead)]
    barrier = pltpu.get_barrier_semaphore()
    for peer in peers:
        pl.semaphore_signal(barrier, inc=1, device_id=peer, device_id_type=MESH)

    loads[0].wait()
    for m in range(MB):
        day = lax.rem(dates[m] + lead, f_hbm.shape[0])
        shift[m] = jnp.broadcast_to(f_v[pl.ds(day, 1), :], (C, L)).T
    loads[1].wait()
    for m in range(MB):
        for d, r in ((0, 0), (1, ROWS - 1)):
            halo_s[d, m] = (x_v[m, pl.ds(r, C, stride=ROWS), :] + shift[m]).astype(BF16)
    for m in range(MB):
        for r in range(ROWS):
            rounded = (x_v[m, pl.ds(r, C, stride=ROWS), :] + shift[m])
            for cs in (-1, 0, 1):
                view = rolled(rounded, -cs).astype(BF16)
                for rs in (-1, 0, 1):
                    if 0 <= r - rs < ROWS:
                        tap = 3 * (rs + 1) + cs + 1
                        taps[m, tap * C:(tap + 1) * C, (r - rs) * L:(r - rs + 1) * L] = view

    loads[2].wait()
    for i in range(9):
        for j in range(4):
            wt_v[j * 128:(j + 1) * 128, i * 128:(i + 1) * 128] = w_v[i * 128:(i + 1) * 128, j * 128:(j + 1) * 128].T
    loads[3].wait()
    for j in range(4):
        bcol[j * 128:(j + 1) * 128, :] = jnp.broadcast_to(b_v[:, j * 128:(j + 1) * 128], (L, L)).T
    for rs in range(3):
        w_cat[:, rs * H:(rs + 1) * H] = w_v[rs * 384:(rs + 1) * 384, :]
        if rs != 1:
            w_edge[rs // 2 * 384:(rs // 2 + 1) * 384, :] = w_v[rs * 384:(rs + 1) * 384, :]
    pl.semaphore_wait(barrier, len(peers))
    above, below = (lead, lax.rem(tile + TILES - 1, TILES)), (lead, lax.rem(tile + 1, TILES))
    inside = (tile > 0, tile < TILES - 1)
    halo_up = remote(halo_s.at[0], halo_r.at[1], halo_ss.at[0], halo_rs.at[1], above)
    halo_down = remote(halo_s.at[1], halo_r.at[0], halo_ss.at[1], halo_rs.at[0], below)
    halo_up.start()
    halo_down.start()

    for lanes in (slice(0, L), slice((ROWS + 1) * L, (ROWS + 2) * L)):
        pre[:, :, lanes] = jnp.zeros((MB, H, L), BF16)
    bias_acc[...] = jnp.zeros_like(bias_acc)

    @pl.when(lead == 1)
    def _():
        sg_r[...] = jnp.zeros_like(sg_r)

    for load in loads[4:]:
        load.wait()

    def halo_arrived():
        halo_up.wait()
        halo_down.wait()
        for m in range(MB):
            for d, rs, r in ((0, -1, 0), (1, 1, ROWS - 1)):
                row = jnp.where(inside[d], halo_r[d, m].astype(F32), 0.0)
                for cs in (-1, 0, 1):
                    tap = 3 * (rs + 1) + cs + 1
                    taps[m, tap * C:(tap + 1) * C, r * L:(r + 1) * L] = rolled(row, -cs).astype(BF16)

    def forward(m, spans):
        for lo, hi in spans:
            cols = slice(lo * L, hi * L)
            v = dot(wt_v[...], taps[m, :, cols])
            v = v + jnp.concatenate([bcol[...]] * (hi - lo), axis=1)
            v2 = v * v
            t = jnp.tanh(v * (TANH_SCALE * CUBIC_TERM * v2 + TANH_SCALE))
            p = 0.5 * t + 0.5
            out = v * p
            hidden[m, :, cols] = out.astype(BF16)
            slope[m, :, cols] = p + out * (1.0 - p) * (6.0 * TANH_SCALE * CUBIC_TERM * v2 + 2.0 * TANH_SCALE)

    def total_row(m, r):
        return cot_v[m, pl.ds(r, C, stride=ROWS), :] + sg_r[m, r].astype(F32)

    def pre_grads(m, spans):
        land = land_v[...].astype(F32)
        for lo, hi in spans:
            for r in range(lo, hi):
                masked[m, :, r * L:(r + 1) * L] = (total_row(m, r) * land[r:r + 1, :]).astype(BF16)
            cols = slice(lo * L, hi * L)
            grad = dot(wo_v[...], masked[m, :, cols]) * slope[m, :, cols]
            sums = [grad[:, i * L:(i + 1) * L] for i in range(hi - lo)]
            while len(sums) > 1:
                sums = [a + b for a, b in zip(sums[::2], sums[1::2])] + sums[len(sums) // 2 * 2:]
            bias_acc[...] += sums[0]
            pre[m, :, (lo + 1) * L:(hi + 1) * L] = grad.astype(BF16)

    def columns(ref, members, rows, spans, offset):
        parts = [ref[m, rows, (lo + offset) * L:(hi + offset) * L] for m in members for lo, hi in spans]
        return parts[0] if len(parts) == 1 else jnp.concatenate(parts, axis=1)

    def weight_grads(members, spans, first, last=False):
        term = dot_t(columns(hidden, members, slice(None), spans, 0), columns(masked, members, slice(None), spans, 0))
        w2_acc[...] = term if first else w2_acc[...] + term
        if last:
            for j in range(4):
                b_row[:, j * 128:(j + 1) * 128] = jnp.sum(bias_acc[j * 128:(j + 1) * 128, :].T, axis=0, keepdims=True)
        p = columns(pre, members, slice(None), spans, 1)
        for lo, hi in ((0, 3), (3, 6), (6, 8)):
            rows = slice(lo * 144, hi * 144)
            term = dot_t(columns(taps, members, rows, spans, 0), p)
            w1_acc[rows, :] = term if first else w1_acc[rows, :] + term
            if last:
                for b in range(lo, hi):
                    start_core_stage(b)

    def gather_steps(acc, lanes):
        return rolled(acc[:C, lanes], -1) + acc[C:2 * C, lanes] + rolled(acc[2 * C:, lanes], 1)

    def conv_edges(m):
        both = dot(w_edge[...], jnp.concatenate([pre[m, :, L:2 * L], pre[m, :, ROWS * L:(ROWS + 1) * L]], axis=1))
        return gather_steps(both[:384], slice(0, L)), gather_steps(both[384:], slice(L, 2 * L))

    def conv_back(m, spans):
        sides = [columns(pre, (m,), slice(None), spans, 1 - rs) for rs in (-1, 0, 1)]
        acc = dot(w_cat[...], jnp.concatenate(sides, axis=0))
        rows = [r for lo, hi in spans for r in range(lo, hi)]
        return [(r, gather_steps(acc, slice(i * L, (i + 1) * L))) for i, r in enumerate(rows)]

    def edges(m):
        up = remote(edge_s.at[m, 0], edge_r.at[m, 1], edge_ss.at[m, 0], edge_rs.at[m, 1], above)
        down = remote(edge_s.at[m, 1], edge_r.at[m, 0], edge_ss.at[m, 1], edge_rs.at[m, 0], below)
        return up, down

    def sg_copy(m, i):
        rows = pl.ds(*((3, 2), (1, 2), (5, 2), (0, 1), (ROWS - 1, 1))[i])
        return remote(sg_s.at[m, rows], sg_r.at[m, rows], sg_ss.at[m, i], sg_rs.at[m, i], (1 - lead, tile))

    def finish_row(m, r, value):
        out_v[m, pl.ds(r, C, stride=ROWS), :] = value
        sg_s[m, r] = value.astype(BF16)

    def send_edges(m):
        edge_s[m, 0], edge_s[m, 1] = conv_edges(m)
        for copy in edges(m):
            copy.start()

    def input_grads(m, spans):
        for r, grad in conv_back(m, spans):
            if r in (0, ROWS - 1):
                part[m, r // (ROWS - 1)] = total_row(m, r) + grad
            else:
                finish_row(m, r, total_row(m, r) + grad)

    def finish_edges(m):
        for copy in edges(m):
            copy.wait()
        for d, r in ((0, 0), (1, ROWS - 1)):
            finish_row(m, r, part[m, d] + jnp.where(inside[d], edge_r[m, d], 0.0))

    def piece(b, half):
        first = b * 64
        return (
            w1_acc[pl.ds(aligned(b * 144, 8), 144), pl.ds(pl.multiple_of(half * 256, 256), 256)],
            jnp.concatenate(
                [
                    jnp.concatenate([w2_acc[pl.ds(aligned(first + 32 * i + 16 * q, 16), 16), :] for i in range(2)], axis=0)
                    for q in range(2)
                ],
                axis=1,
            ),
            jnp.broadcast_to(b_row[:, pl.ds(pl.multiple_of(half * 256, 256), 256)], (8, 256)),
        )

    pair = (lead, tile + 1 - 2 * core)

    def c_copy(b):
        return remote(c_s.at[b], c_r.at[b], c_ss.at[b], c_rs.at[b], pair)

    def y_copy(k):
        b = lax.rem(block + 1 + k, BLOCKS)
        return b, remote(y_s.at[b], y_r.at[k], y_ss.at[k], y_rs.at[k], (lead, b * LOCAL + local))

    def start_core_stage(b):
        for value, lo, hi in zip(piece(b, 1 - core), (0, 144, 176), (144, 176, BROWS)):
            c_s[b, lo:hi, :] = value.astype(BF16)
        c_copy(b).start()

    inner, outer, whole = ((2, 6),), ((0, 2), (6, 8)), ((0, 4), (4, 8))
    most, ends = ((1, 7),), ((0, 1), (7, 8))

    @pl.when(lead == 1)
    def _():
        for m in range(MB):
            forward(m, inner)
            pre_grads(m, inner)
            input_grads(m, ((3, 5),))
            sg_copy(m, 0).start()
        halo_arrived()
        for m in range(MB):
            forward(m, outer)
            pre_grads(m, outer)
            if m == MB - 1:
                send_edges(m)
            input_grads(m, ((1, 3), (5, 7)))
            for i in (1, 2):
                sg_copy(m, i).start()
            if m < MB - 1:
                send_edges(m)
        for m in range(MB):
            input_grads(m, ends)
        for m in range(MB):
            finish_edges(m)
            for i in (3, 4):
                sg_copy(m, i).start()
        for m in range(MB):
            weight_grads((m,), ((0, 8),), m == 0, m == MB - 1)

    @pl.when(lead == 0)
    def _():
        for m in range(MB):
            forward(m, inner)
        halo_arrived()
        for m in range(MB):
            forward(m, outer)
        for m in range(MB):
            for i in range(3):
                sg_copy(m, i).wait_recv()
            pre_grads(m, most)
            weight_grads((m,), most, m == 0)
        for m in range(MB):
            for i in (3, 4):
                sg_copy(m, i).wait_recv()
            pre_grads(m, ends)
        weight_grads((0, 1), ends, False, True)

    @pl.when(lead == 0)
    def _():
        for m in range(MB):
            send_edges(m)

    def x_copy(k):
        to = lax.rem(xpos + k, 4)
        return remote(x_s.at[to], x_r.at[k - 1], x_ss.at[k - 1], x_rs.at[k - 1], (lead, block * LOCAL + 2 * to + 1))

    xrow_id = lax.broadcasted_iota(jnp.int32, (XROWS, 256), 0)
    row_id = lax.broadcasted_iota(jnp.int32, (24, 256), 0)

    @pl.when(core == 0)
    def _():
        for k in range(BLOCKS):
            b = lax.rem(block + 1 + k, BLOCKS)
            c_copy(b).wait_recv()
            for value, lo, hi in zip(piece(b, 0), (0, 144, 176), (144, 176, BROWS)):
                value = value + c_r[b, lo:hi, :].astype(F32)
                if k < BLOCKS - 1:
                    y_s[b, lo:hi, :] = value.astype(BF16)
                else:
                    y_sum[lo:hi, :] = value
            if k < BLOCKS - 1:
                y_copy(k)[1].start()

    @pl.when(core == 1)
    def _():
        for b in range(BLOCKS):
            c_copy(b).wait_recv()
            w1_part, _, bias = piece(b, 1)
            x_t[b, :144, :] = w1_part + c_r[b, :144, :].astype(F32)
            x_t[b, 144:152, :] = bias + c_r[b, 176:, :].astype(F32)
            for x in range(4):
                rows = jnp.where(xrow_id == 36, x_t[b, 144:145, :], x_t[b, 36 * x:36 * x + XROWS, :])
                x_s[x, b] = rows.astype(BF16)
        for k in (2, 1, 3):
            x_copy(k).start()

    @pl.when(lead == 0)
    def _():
        for m in range(MB):
            for span in whole:
                input_grads(m, (span,))
        for m in range(MB):
            finish_edges(m)

    l0_copy = remote(l0_s, l0_r, l_ss.at[0], l_rs.at[0], (1 - lead, tile))
    l1_copy = remote(l1_s, l1_r, l_ss.at[1], l_rs.at[1], (1 - lead, tile))

    def f_copy(k, which):
        to = lax.rem(local + k, LOCAL)
        return remote(f_s.at[to], f_r.at[xpos], f_ss.at[k, which], f_rs.at[xpos], (which, block * LOCAL + to))

    def g_copy(k, c, which):
        to = lax.rem(block + k, BLOCKS)
        return remote(
            g_s.at[c, to], g_r.at[block], g_ss.at[k, 2 * c + which], g_rs.at[block], (which, to * LOCAL + 2 * xpos + c)
        )

    @pl.when(core == 0)
    def _():
        for k in range(BLOCKS - 1):
            y_copy(k)[1].wait_recv()
            y_sum[...] += y_r[k].astype(F32)

        @pl.when(lead == 1)
        def _():
            l0_s[...] = y_sum[...].astype(BF16)
            l0_copy.start()

        @pl.when(lead == 0)
        def _():
            l0_copy.wait_recv()
            y_sum[...] += l0_r[...].astype(F32)
            for j in range(LOCAL):
                f_t[j, :18, :] = y_sum[18 * j:18 * j + 18, :]
                f_t[j, 18:19, :] = y_sum[176:177, :]
                x, c = j // 2, j % 2
                for i in range(2):
                    first = 144 + 16 * (x // 2) + 8 * c + 4 * i
                    f_t[j, 19:23, i * L:(i + 1) * L] = y_sum[first:first + 4, (x % 2) * L:(x % 2 + 1) * L]
                f_t[j, 23:24, :] = jnp.zeros((1, 256), F32)
                f_s[j] = f_t[j].astype(BF16)
            for k in range(LOCAL):
                f_copy(k, 1).start()
            for k in range(1, LOCAL):
                f_copy(k, 0).start()
            f_r[xpos] = f_s[local]

    @pl.when(core == 1)
    def _():
        for k in range(1, 4):
            x_copy(k).wait_recv()
        for b in range(BLOCKS):
            total = x_s[xpos, b].astype(F32)
            for k in range(3):
                total = total + x_r[k, b].astype(F32)
            x_t[b, :XROWS, :] = total

        @pl.when(lead == 1)
        def _():
            l1_s[...] = x_t[:, :XROWS, :].astype(BF16)
            l1_copy.start()

        @pl.when(lead == 0)
        def _():
            l1_copy.wait_recv()
            for b in range(BLOCKS):
                x_t[b, :XROWS, :] = x_t[b, :XROWS, :] + l1_r[b].astype(F32)
                for c in range(2):
                    rows = jnp.where(row_id == 18, x_t[b, 36:37, :], x_t[b, 18 * c:18 * c + 24, :])
                    g_s[c, b] = rows.astype(BF16)
            for k in range(BLOCKS):
                for c in range(2):
                    g_copy(k, c, 1).start()
            g_copy(0, 0, 0).start()
            for k in range(1, BLOCKS):
                for c in range(2):
                    g_copy(k, c, 0).start()
            g_r[block] = g_s[1, block]

    def f_landed(k):
        source = lax.rem(xpos + k, 4)
        return remote(f_s.at[0], f_r.at[source], f_ss.at[0, 0], f_rs.at[source], (1 - lead, tile))

    def g_landed(k):
        source = lax.rem(block + k, BLOCKS)
        return remote(g_s.at[0, 0], g_r.at[source], g_ss.at[0, 0], g_rs.at[source], (1 - lead, tile))

    @pl.when((lead == 1) | (core == 1))
    def _():
        f_landed(0).wait_recv()

    @pl.when((lead == 1) | (core == 0))
    def _():
        g_landed(0).wait_recv()

    for k in range(1, 4):
        f_landed(k).wait_recv()
    for k in range(1, BLOCKS):
        g_landed(k).wait_recv()

    total = f_r[0].astype(F32)
    for x in range(1, 4):
        total = total + f_r[x].astype(F32)
    total = total * scale
    w1_out[:, :256] = total[:18]
    b_row[:, :256] = total[18:19]
    w2_out[:4, :] = total[19:23, :L]
    w2_out[4:, :] = total[19:23, L:]
    total = g_r[0].astype(F32)
    for b in range(1, BLOCKS):
        total = total + g_r[b].astype(F32)
    total = total * scale
    w1_out[:, 256:] = total[:18]
    b_row[:, 256:] = total[18:19]
    b1 = b_row[:, :L]
    for q in range(1, 4):
        b1 = jnp.where(lax.div(tile, 16) == q, b_row[:, q * L:(q + 1) * L], b1)
    b1_out[...] = pltpu.roll(b1, lax.rem(L - 8 * lax.rem(tile, 16), L), 1)

    @pl.when(lead == 1)
    def _():
        for m in range(MB):
            for i in range(5):
                sg_copy(m, i).wait_send()

    for b in range(BLOCKS):
        c_copy(b).wait_send()

    @pl.when(core == 0)
    def _():
        for k in range(BLOCKS - 1):
            y_copy(k)[1].wait_send()

        @pl.when(lead == 1)
        def _():
            l0_copy.wait_send()

        @pl.when(lead == 0)
        def _():
            for k in range(LOCAL):
                f_copy(k, 1).wait_send()
            for k in range(1, LOCAL):
                f_copy(k, 0).wait_send()

    @pl.when(core == 1)
    def _():
        for k in range(1, 4):
            x_copy(k).wait_send()

        @pl.when(lead == 1)
        def _():
            l1_copy.wait_send()

        @pl.when(lead == 0)
        def _():
            for k in range(BLOCKS):
                for c in range(2):
                    g_copy(k, c, 1).wait_send()
            g_copy(0, 0, 0).wait_send()
            for k in range(1, BLOCKS):
                for c in range(2):
                    g_copy(k, c, 0).wait_send()


def deliver(*refs):
    held, outs, b1_own, sems = refs[:4], refs[4:8], refs[8], refs[9]
    b1_own[...] = held[3][0, :8]
    held = held[:3] + (b1_own,)
    copies = [pltpu.make_async_copy(src, dst, sems.at[i]) for i, (src, dst) in enumerate(zip(held, outs))]
    for copy in copies:
        copy.start()
    for copy in copies:
        copy.wait()


def shards(states, cotangents, w_conv, b_conv, w_out, forcing, land, dates):
    grad_scale = 1.0 / math.sqrt(2 * MB * TILES * ROWS * L)
    any_spec = pl.BlockSpec(memory_space=pl.ANY)
    vmem_spec = pl.BlockSpec(memory_space=pltpu.VMEM)
    dma = pltpu.SemaphoreType.DMA
    flat = (MB, C * ROWS, L)
    out, w1, w2, b1 = pl.pallas_call(
        functools.partial(kernel, grad_scale),
        out_shape=(
            pltpu.VMEM(flat, F32),
            pltpu.VMEM((18, H), F32),
            pltpu.VMEM((8, C), F32),
            pltpu.VMEM((1, L), F32),
        ),
        in_specs=[pl.BlockSpec(memory_space=pltpu.SMEM)] + [any_spec] * 7,
        out_specs=(vmem_spec, vmem_spec, vmem_spec, vmem_spec),
        scratch_shapes=[
            pltpu.VMEM(flat, F32),
            pltpu.VMEM(flat, F32),
            pltpu.VMEM((9 * C, H), BF16),
            pltpu.VMEM((H, 9 * C), BF16),
            pltpu.VMEM((3 * C, 3 * H), BF16),
            pltpu.VMEM((6 * C, H), BF16),
            pltpu.VMEM((1, H), F32),
            pltpu.VMEM((H, C), BF16),
            pltpu.VMEM(forcing.shape, F32),
            pltpu.VMEM((ROWS, L), jnp.int32),
            pltpu.VMEM((H, L), F32),
            pltpu.VMEM((MB, C, L), F32),
            pltpu.VMEM((MB, 9 * C, ROWS * L), BF16),
            pltpu.VMEM((2, MB, C, L), BF16),
            pltpu.VMEM((2, MB, C, L), BF16),
            pltpu.VMEM((MB, H, ROWS * L), BF16),
            pltpu.VMEM((MB, H, ROWS * L), F32),
            pltpu.VMEM((MB, C, ROWS * L), BF16),
            pltpu.VMEM((MB, H, (ROWS + 2) * L), BF16),
            pltpu.VMEM((H, L), F32),
            pltpu.VMEM((MB, 2, C, L), F32),
            pltpu.VMEM((MB, 2, C, L), F32),
            pltpu.VMEM((MB, 2, C, L), F32),
            pltpu.VMEM((MB, ROWS, C, L), BF16),
            pltpu.VMEM((MB, ROWS, C, L), BF16),
            pltpu.VMEM((9 * C, H), F32),
            pltpu.VMEM((H, C), F32),
            pltpu.VMEM((1, H), F32),
            pltpu.VMEM((BLOCKS, BROWS, 256), BF16),
            pltpu.VMEM((BLOCKS, BROWS, 256), BF16),
            pltpu.VMEM((BLOCKS, BROWS, 256), BF16),
            pltpu.VMEM((BLOCKS - 1, BROWS, 256), BF16),
            pltpu.VMEM((BROWS, 256), F32),
            pltpu.VMEM((LOCAL, 24, 256), F32),
            pltpu.VMEM((LOCAL, 24, 256), BF16),
            pltpu.VMEM((4, 24, 256), BF16),
            pltpu.VMEM((BROWS, 256), BF16),
            pltpu.VMEM((BROWS, 256), BF16),
            pltpu.VMEM((4, BLOCKS, XROWS, 256), BF16),
            pltpu.VMEM((3, BLOCKS, XROWS, 256), BF16),
            pltpu.VMEM((BLOCKS, 152, 256), F32),
            pltpu.VMEM((2, BLOCKS, 24, 256), BF16),
            pltpu.VMEM((BLOCKS, 24, 256), BF16),
            pltpu.VMEM((BLOCKS, XROWS, 256), BF16),
            pltpu.VMEM((BLOCKS, XROWS, 256), BF16),
            dma((7,)), dma((2,)), dma((2,)), dma((MB, 2)), dma((MB, 2)), dma((MB, 5)), dma((MB, 5)),
            dma((BLOCKS,)), dma((BLOCKS,)), dma((BLOCKS - 1,)), dma((BLOCKS - 1,)), dma((LOCAL, 2)), dma((4,)), dma((3,)), dma((3,)), dma((BLOCKS, 4)), dma((BLOCKS,)), dma((2,)), dma((2,)),
        ],
        compiler_params=pltpu.CompilerParams(collective_id=0, has_side_effects=True, vmem_limit_bytes=56 << 20),
    )(
        dates,
        states.reshape(flat),
        cotangents.reshape(flat),
        w_conv,
        b_conv.reshape(1, H),
        w_out,
        forcing,
        land,
    )
    out, w1, w2, b1 = pl.pallas_call(
        deliver,
        out_shape=(
            jax.ShapeDtypeStruct(flat, F32),
            jax.ShapeDtypeStruct((18, H), F32),
            jax.ShapeDtypeStruct((8, C), F32),
            jax.ShapeDtypeStruct((8,), F32),
        ),
        in_specs=[vmem_spec] * 4,
        out_specs=(any_spec,) * 4,
        scratch_shapes=[pltpu.VMEM((8,), F32), dma((4,))],
    )(*(pltpu.with_memory_space_constraint(value, pltpu.VMEM) for value in (out, w1, w2, b1)))
    return out.reshape(states.shape), w1, w2, b1


def solution(mesh):
    placed = (
        P("lead", None, None, "tile", None),
        P("lead", None, None, "tile", None),
        P(),
        P(),
        P(),
        P(),
        P("tile", None),
        P(),
    )
    return jax.shard_map(
        shards,
        mesh=mesh,
        in_specs=placed,
        out_specs=(
            P("lead", None, None, "tile", None),
            P("tile", None),
            P("tile", None),
            P("tile"),
        ),
        check_vma=False,
    )
```

```python
import functools
import math

import jax
import jax.numpy as jnp
from jax import lax
from jax.experimental import pallas as pl
from jax.experimental.pallas import tpu as pltpu
from jax.sharding import PartitionSpec as P

MESH = pl.DeviceIdType.MESH
TANH_SCALE = 0.7978845608028654
CUBIC_TERM = 0.044715
F32 = jnp.float32
BF16 = jnp.bfloat16

C = 128
H = 512
ROWS = 8
L = 128
MB = 2
TILES = 64
BLOCKS = 8
LOCAL = 8
BROWS = 184
XROWS = 40


def remote(src, dst, send_sem, recv_sem, device):
    return pltpu.make_async_remote_copy(
        src_ref=src, dst_ref=dst, send_sem=send_sem, recv_sem=recv_sem,
        device_id=device, device_id_type=MESH,
    )


def dot(a, b):
    return jnp.dot(a, b, preferred_element_type=F32)


def dot_t(a, b):
    return lax.dot_general(a, b, (((1,), (1,)), ((), ())), preferred_element_type=F32)


def aligned(index, size):
    return index if isinstance(index, int) else pl.multiple_of(index, size)


def rolled(value, shift):
    return value if shift % L == 0 else pltpu.roll(value, shift % L, 1)


def kernel(
    scale,
    dates, x_hbm, cot_hbm, w_hbm, b_hbm, wo_hbm, f_hbm, land_hbm,
    out_v, w1_out, w2_out, b1_out,
    x_v, cot_v, w_v, wt_v, w_cat, w_edge, b_v, wo_v, f_v, land_v,
    bcol, shift, taps, halo_s, halo_r, hidden, slope, masked, pre, bias_acc,
    edge_s, edge_r, part, sg_s, sg_r, w1_acc, w2_acc, b_row,
    c_s, c_r, y_s, y_r, y_sum, f_t, f_s, f_r, l0_s, l0_r, x_s, x_r, x_t, g_s, g_r, l1_s, l1_r,
    in_sem, halo_ss, halo_rs, edge_ss, edge_rs, sg_ss, sg_rs,
    c_ss, c_rs, y_ss, y_rs, f_ss, f_rs, x_ss, x_rs, g_ss, g_rs, l_ss, l_rs,
):
    lead = lax.axis_index("lead")
    tile = lax.axis_index("tile")
    core = lax.rem(tile, 2)
    local = lax.rem(tile, LOCAL)
    block = lax.div(tile, LOCAL)
    xpos = lax.div(local, 2)

    loads = [
        pltpu.make_async_copy(src, dst, in_sem.at[i])
        for i, (src, dst) in enumerate(
            [(f_hbm, f_v), (x_hbm, x_v), (w_hbm, w_v), (b_hbm, b_v), (cot_hbm, cot_v), (land_hbm, land_v), (wo_hbm, wo_v)]
        )
    ]
    for load in loads:
        load.start()

    peers = [(lead, lax.rem(tile + 1, TILES)), (lead, lax.rem(tile + TILES - 1, TILES)), (1 - lead, tile)]
    others = [lax.rem(block + k, BLOCKS) * LOCAL + 2 * xpos + c for k in range(1, BLOCKS) for c in range(2)]
    others += [block * LOCAL + lax.rem(local + k, LOCAL) for k in range(1, LOCAL)]
    peers += [(which, other) for other in others for which in (lead, 1 - lead)]
    barrier = pltpu.get_barrier_semaphore()
    for peer in peers:
        pl.semaphore_signal(barrier, inc=1, device_id=peer, device_id_type=MESH)

    loads[0].wait()
    for m in range(MB):
        day = lax.rem(dates[m] + lead, f_hbm.shape[0])
        shift[m] = jnp.broadcast_to(f_v[pl.ds(day, 1), :], (C, L)).T
    loads[1].wait()
    for m in range(MB):
        for d, r in ((0, 0), (1, ROWS - 1)):
            halo_s[d, m] = (x_v[m, pl.ds(r, C, stride=ROWS), :] + shift[m]).astype(BF16)
    for m in range(MB):
        for r in range(ROWS):
            rounded = (x_v[m, pl.ds(r, C, stride=ROWS), :] + shift[m])
            for cs in (-1, 0, 1):
                view = rolled(rounded, -cs).astype(BF16)
                for rs in (-1, 0, 1):
                    if 0 <= r - rs < ROWS:
                        tap = 3 * (rs + 1) + cs + 1
                        taps[m, tap * C:(tap + 1) * C, (r - rs) * L:(r - rs + 1) * L] = view

    loads[2].wait()
    for i in range(9):
        for j in range(4):
            wt_v[j * 128:(j + 1) * 128, i * 128:(i + 1) * 128] = w_v[i * 128:(i + 1) * 128, j * 128:(j + 1) * 128].T
    loads[3].wait()
    for j in range(4):
        bcol[j * 128:(j + 1) * 128, :] = jnp.broadcast_to(b_v[:, j * 128:(j + 1) * 128], (L, L)).T
    for rs in range(3):
        w_cat[:, rs * H:(rs + 1) * H] = w_v[rs * 384:(rs + 1) * 384, :]
        if rs != 1:
            w_edge[rs // 2 * 384:(rs // 2 + 1) * 384, :] = w_v[rs * 384:(rs + 1) * 384, :]
    pl.semaphore_wait(barrier, len(peers))
    above, below = (lead, lax.rem(tile + TILES - 1, TILES)), (lead, lax.rem(tile + 1, TILES))
    inside = (tile > 0, tile < TILES - 1)
    halo_up = remote(halo_s.at[0], halo_r.at[1], halo_ss.at[0], halo_rs.at[1], above)
    halo_down = remote(halo_s.at[1], halo_r.at[0], halo_ss.at[1], halo_rs.at[0], below)
    halo_up.start()
    halo_down.start()

    for lanes in (slice(0, L), slice((ROWS + 1) * L, (ROWS + 2) * L)):
        pre[:, :, lanes] = jnp.zeros((MB, H, L), BF16)
    bias_acc[...] = jnp.zeros_like(bias_acc)

    @pl.when(lead == 1)
    def _():
        sg_r[...] = jnp.zeros_like(sg_r)

    for load in loads[4:]:
        load.wait()

    def halo_arrived():
        halo_up.wait()
        halo_down.wait()
        for m in range(MB):
            for d, rs, r in ((0, -1, 0), (1, 1, ROWS - 1)):
                row = jnp.where(inside[d], halo_r[d, m].astype(F32), 0.0)
                for cs in (-1, 0, 1):
                    tap = 3 * (rs + 1) + cs + 1
                    taps[m, tap * C:(tap + 1) * C, r * L:(r + 1) * L] = rolled(row, -cs).astype(BF16)

    def forward(m, spans):
        for lo, hi in spans:
            cols = slice(lo * L, hi * L)
            v = dot(wt_v[...], taps[m, :, cols])
            v = v + jnp.concatenate([bcol[...]] * (hi - lo), axis=1)
            v2 = v * v
            t = jnp.tanh(v * (TANH_SCALE * CUBIC_TERM * v2 + TANH_SCALE))
            p = 0.5 * t + 0.5
            out = v * p
            hidden[m, :, cols] = out.astype(BF16)
            slope[m, :, cols] = p + out * (1.0 - p) * (6.0 * TANH_SCALE * CUBIC_TERM * v2 + 2.0 * TANH_SCALE)

    def total_row(m, r):
        return cot_v[m, pl.ds(r, C, stride=ROWS), :] + sg_r[m, r].astype(F32)

    def pre_grads(m, spans):
        land = land_v[...].astype(F32)
        for lo, hi in spans:
            for r in range(lo, hi):
                masked[m, :, r * L:(r + 1) * L] = (total_row(m, r) * land[r:r + 1, :]).astype(BF16)
            cols = slice(lo * L, hi * L)
            grad = dot(wo_v[...], masked[m, :, cols]) * slope[m, :, cols]
            sums = [grad[:, i * L:(i + 1) * L] for i in range(hi - lo)]
            while len(sums) > 1:
                sums = [a + b for a, b in zip(sums[::2], sums[1::2])] + sums[len(sums) // 2 * 2:]
            bias_acc[...] += sums[0]
            pre[m, :, (lo + 1) * L:(hi + 1) * L] = grad.astype(BF16)

    def columns(ref, members, rows, spans, offset):
        parts = [ref[m, rows, (lo + offset) * L:(hi + offset) * L] for m in members for lo, hi in spans]
        return parts[0] if len(parts) == 1 else jnp.concatenate(parts, axis=1)

    def weight_grads(members, spans, first, last=False):
        term = dot_t(columns(hidden, members, slice(None), spans, 0), columns(masked, members, slice(None), spans, 0))
        w2_acc[...] = term if first else w2_acc[...] + term
        if last:
            for j in range(4):
                b_row[:, j * 128:(j + 1) * 128] = jnp.sum(bias_acc[j * 128:(j + 1) * 128, :].T, axis=0, keepdims=True)
        p = columns(pre, members, slice(None), spans, 1)
        for lo, hi in ((0, 3), (3, 6), (6, 8)):
            rows = slice(lo * 144, hi * 144)
            term = dot_t(columns(taps, members, rows, spans, 0), p)
            w1_acc[rows, :] = term if first else w1_acc[rows, :] + term
            if last:
                for b in range(lo, hi):
                    start_core_stage(b)

    def gather_steps(acc, lanes):
        return rolled(acc[:C, lanes], -1) + acc[C:2 * C, lanes] + rolled(acc[2 * C:, lanes], 1)

    def conv_edges(m):
        both = dot(w_edge[...], jnp.concatenate([pre[m, :, L:2 * L], pre[m, :, ROWS * L:(ROWS + 1) * L]], axis=1))
        return gather_steps(both[:384], slice(0, L)), gather_steps(both[384:], slice(L, 2 * L))

    def conv_back(m, spans):
        sides = [columns(pre, (m,), slice(None), spans, 1 - rs) for rs in (-1, 0, 1)]
        acc = dot(w_cat[...], jnp.concatenate(sides, axis=0))
        rows = [r for lo, hi in spans for r in range(lo, hi)]
        return [(r, gather_steps(acc, slice(i * L, (i + 1) * L))) for i, r in enumerate(rows)]

    def edges(m):
        up = remote(edge_s.at[m, 0], edge_r.at[m, 1], edge_ss.at[m, 0], edge_rs.at[m, 1], above)
        down = remote(edge_s.at[m, 1], edge_r.at[m, 0], edge_ss.at[m, 1], edge_rs.at[m, 0], below)
        return up, down

    def sg_copy(m, i):
        rows = pl.ds(*((3, 2), (1, 2), (5, 2), (0, 1), (ROWS - 1, 1))[i])
        return remote(sg_s.at[m, rows], sg_r.at[m, rows], sg_ss.at[m, i], sg_rs.at[m, i], (1 - lead, tile))

    def finish_row(m, r, value):
        out_v[m, pl.ds(r, C, stride=ROWS), :] = value
        sg_s[m, r] = value.astype(BF16)

    def send_edges(m):
        for d, row in enumerate(conv_edges(m)):
            edge_s[m, d] = row.astype(BF16)
        for copy in edges(m):
            copy.start()

    def input_grads(m, spans):
        for r, grad in conv_back(m, spans):
            if r in (0, ROWS - 1):
                part[m, r // (ROWS - 1)] = total_row(m, r) + grad
            else:
                finish_row(m, r, total_row(m, r) + grad)

    def finish_edges(m):
        for copy in edges(m):
            copy.wait()
        for d, r in ((0, 0), (1, ROWS - 1)):
            finish_row(m, r, part[m, d] + jnp.where(inside[d], edge_r[m, d].astype(F32), 0.0))

    def piece(b, half):
        first = b * 64
        return (
            w1_acc[pl.ds(aligned(b * 144, 8), 144), pl.ds(pl.multiple_of(half * 256, 256), 256)],
            jnp.concatenate(
                [
                    jnp.concatenate([w2_acc[pl.ds(aligned(first + 32 * i + 16 * q, 16), 16), :] for i in range(2)], axis=0)
                    for q in range(2)
                ],
                axis=1,
            ),
            jnp.broadcast_to(b_row[:, pl.ds(pl.multiple_of(half * 256, 256), 256)], (8, 256)),
        )

    pair = (lead, tile + 1 - 2 * core)

    def c_copy(b):
        return remote(c_s.at[b], c_r.at[b], c_ss.at[b], c_rs.at[b], pair)

    def y_copy(k):
        b = lax.rem(block + 1 + k, BLOCKS)
        return b, remote(y_s.at[b], y_r.at[k], y_ss.at[k], y_rs.at[k], (lead, b * LOCAL + local))

    def start_core_stage(b):
        for value, lo, hi in zip(piece(b, 1 - core), (0, 144, 176), (144, 176, BROWS)):
            c_s[b, lo:hi, :] = value.astype(BF16)
        c_copy(b).start()

    inner, outer, whole = ((2, 6),), ((0, 2), (6, 8)), ((0, 4), (4, 8))
    most, ends = ((1, 7),), ((0, 1), (7, 8))

    @pl.when(lead == 1)
    def _():
        for m in range(MB):
            forward(m, inner)
            pre_grads(m, inner)
            input_grads(m, ((3, 5),))
            sg_copy(m, 0).start()
        halo_arrived()
        for m in range(MB):
            forward(m, outer)
            pre_grads(m, outer)
            if m == MB - 1:
                send_edges(m)
            input_grads(m, ((1, 3), (5, 7)))
            for i in (1, 2):
                sg_copy(m, i).start()
            if m < MB - 1:
                send_edges(m)
        for m in range(MB):
            input_grads(m, ends)
        for m in range(MB):
            finish_edges(m)
            for i in (3, 4):
                sg_copy(m, i).start()
        for m in range(MB):
            weight_grads((m,), ((0, 8),), m == 0, m == MB - 1)

    @pl.when(lead == 0)
    def _():
        for m in range(MB):
            forward(m, inner)
        halo_arrived()
        for m in range(MB):
            forward(m, outer)
        for m in range(MB):
            for i in range(3):
                sg_copy(m, i).wait_recv()
            pre_grads(m, most)
            weight_grads((m,), most, m == 0)
        for m in range(MB):
            for i in (3, 4):
                sg_copy(m, i).wait_recv()
            pre_grads(m, ends)
        weight_grads((0, 1), ends, False, True)

    @pl.when(lead == 0)
    def _():
        for m in range(MB):
            send_edges(m)

    def x_copy(k):
        to = lax.rem(xpos + k, 4)
        return remote(x_s.at[to], x_r.at[k - 1], x_ss.at[k - 1], x_rs.at[k - 1], (lead, block * LOCAL + 2 * to + 1))

    xrow_id = lax.broadcasted_iota(jnp.int32, (XROWS, 256), 0)
    row_id = lax.broadcasted_iota(jnp.int32, (24, 256), 0)

    @pl.when(core == 0)
    def _():
        for k in range(BLOCKS):
            b = lax.rem(block + 1 + k, BLOCKS)
            c_copy(b).wait_recv()
            for value, lo, hi in zip(piece(b, 0), (0, 144, 176), (144, 176, BROWS)):
                value = value + c_r[b, lo:hi, :].astype(F32)
                if k < BLOCKS - 1:
                    y_s[b, lo:hi, :] = value.astype(BF16)
                else:
                    y_sum[lo:hi, :] = value
            if k < BLOCKS - 1:
                y_copy(k)[1].start()

    @pl.when(core == 1)
    def _():
        for b in range(BLOCKS):
            c_copy(b).wait_recv()
            w1_part, _, bias = piece(b, 1)
            x_t[b, :144, :] = w1_part + c_r[b, :144, :].astype(F32)
            x_t[b, 144:152, :] = bias + c_r[b, 176:, :].astype(F32)
            for x in range(4):
                rows = jnp.where(xrow_id == 36, x_t[b, 144:145, :], x_t[b, 36 * x:36 * x + XROWS, :])
                x_s[x, b] = rows.astype(BF16)
        for k in (2, 1, 3):
            x_copy(k).start()

    @pl.when(lead == 0)
    def _():
        for m in range(MB):
            for span in whole:
                input_grads(m, (span,))
        for m in range(MB):
            finish_edges(m)

    l0_copy = remote(l0_s, l0_r, l_ss.at[0], l_rs.at[0], (1 - lead, tile))
    l1_copy = remote(l1_s, l1_r, l_ss.at[1], l_rs.at[1], (1 - lead, tile))

    def f_copy(k, which):
        to = lax.rem(local + k, LOCAL)
        return remote(f_s.at[to], f_r.at[xpos], f_ss.at[k, which], f_rs.at[xpos], (which, block * LOCAL + to))

    def g_copy(k, c, which):
        to = lax.rem(block + k, BLOCKS)
        return remote(
            g_s.at[c, to], g_r.at[block], g_ss.at[k, 2 * c + which], g_rs.at[block], (which, to * LOCAL + 2 * xpos + c)
        )

    @pl.when(core == 0)
    def _():
        for k in range(BLOCKS - 1):
            y_copy(k)[1].wait_recv()
            y_sum[...] += y_r[k].astype(F32)

        @pl.when(lead == 1)
        def _():
            l0_s[...] = y_sum[...].astype(BF16)
            l0_copy.start()

        @pl.when(lead == 0)
        def _():
            l0_copy.wait_recv()
            y_sum[...] += l0_r[...].astype(F32)
            for j in range(LOCAL):
                f_t[j, :18, :] = y_sum[18 * j:18 * j + 18, :]
                f_t[j, 18:19, :] = y_sum[176:177, :]
                x, c = j // 2, j % 2
                for i in range(2):
                    first = 144 + 16 * (x // 2) + 8 * c + 4 * i
                    f_t[j, 19:23, i * L:(i + 1) * L] = y_sum[first:first + 4, (x % 2) * L:(x % 2 + 1) * L]
                f_t[j, 23:24, :] = jnp.zeros((1, 256), F32)
                f_s[j] = f_t[j].astype(BF16)
            for k in range(LOCAL):
                f_copy(k, 1).start()
            for k in range(1, LOCAL):
                f_copy(k, 0).start()
            f_r[xpos] = f_s[local]

    @pl.when(core == 1)
    def _():
        for k in range(1, 4):
            x_copy(k).wait_recv()
        for b in range(BLOCKS):
            total = x_s[xpos, b].astype(F32)
            for k in range(3):
                total = total + x_r[k, b].astype(F32)
            x_t[b, :XROWS, :] = total

        @pl.when(lead == 1)
        def _():
            l1_s[...] = x_t[:, :XROWS, :].astype(BF16)
            l1_copy.start()

        @pl.when(lead == 0)
        def _():
            l1_copy.wait_recv()
            for b in range(BLOCKS):
                x_t[b, :XROWS, :] = x_t[b, :XROWS, :] + l1_r[b].astype(F32)
                for c in range(2):
                    rows = jnp.where(row_id == 18, x_t[b, 36:37, :], x_t[b, 18 * c:18 * c + 24, :])
                    g_s[c, b] = rows.astype(BF16)
            for k in range(BLOCKS):
                for c in range(2):
                    g_copy(k, c, 1).start()
            g_copy(0, 0, 0).start()
            for k in range(1, BLOCKS):
                for c in range(2):
                    g_copy(k, c, 0).start()
            g_r[block] = g_s[1, block]

    def f_landed(k):
        source = lax.rem(xpos + k, 4)
        return remote(f_s.at[0], f_r.at[source], f_ss.at[0, 0], f_rs.at[source], (1 - lead, tile))

    def g_landed(k):
        source = lax.rem(block + k, BLOCKS)
        return remote(g_s.at[0, 0], g_r.at[source], g_ss.at[0, 0], g_rs.at[source], (1 - lead, tile))

    @pl.when((lead == 1) | (core == 1))
    def _():
        f_landed(0).wait_recv()

    @pl.when((lead == 1) | (core == 0))
    def _():
        g_landed(0).wait_recv()

    for k in range(1, 4):
        f_landed(k).wait_recv()
    for k in range(1, BLOCKS):
        g_landed(k).wait_recv()

    total = f_r[0].astype(F32)
    for x in range(1, 4):
        total = total + f_r[x].astype(F32)
    total = total * scale
    w1_out[:, :256] = total[:18]
    b_row[:, :256] = total[18:19]
    w2_out[:4, :] = total[19:23, :L]
    w2_out[4:, :] = total[19:23, L:]
    total = g_r[0].astype(F32)
    for b in range(1, BLOCKS):
        total = total + g_r[b].astype(F32)
    total = total * scale
    w1_out[:, 256:] = total[:18]
    b_row[:, 256:] = total[18:19]
    b1 = b_row[:, :L]
    for q in range(1, 4):
        b1 = jnp.where(lax.div(tile, 16) == q, b_row[:, q * L:(q + 1) * L], b1)
    b1_out[...] = pltpu.roll(b1, lax.rem(L - 8 * lax.rem(tile, 16), L), 1)

    @pl.when(lead == 1)
    def _():
        for m in range(MB):
            for i in range(5):
                sg_copy(m, i).wait_send()

    for b in range(BLOCKS):
        c_copy(b).wait_send()

    @pl.when(core == 0)
    def _():
        for k in range(BLOCKS - 1):
            y_copy(k)[1].wait_send()

        @pl.when(lead == 1)
        def _():
            l0_copy.wait_send()

        @pl.when(lead == 0)
        def _():
            for k in range(LOCAL):
                f_copy(k, 1).wait_send()
            for k in range(1, LOCAL):
                f_copy(k, 0).wait_send()

    @pl.when(core == 1)
    def _():
        for k in range(1, 4):
            x_copy(k).wait_send()

        @pl.when(lead == 1)
        def _():
            l1_copy.wait_send()

        @pl.when(lead == 0)
        def _():
            for k in range(BLOCKS):
                for c in range(2):
                    g_copy(k, c, 1).wait_send()
            g_copy(0, 0, 0).wait_send()
            for k in range(1, BLOCKS):
                for c in range(2):
                    g_copy(k, c, 0).wait_send()


def deliver(*refs):
    held, outs, b1_own, sems = refs[:4], refs[4:8], refs[8], refs[9]
    b1_own[...] = held[3][0, :8]
    held = held[:3] + (b1_own,)
    copies = [pltpu.make_async_copy(src, dst, sems.at[i]) for i, (src, dst) in enumerate(zip(held, outs))]
    for copy in copies:
        copy.start()
    for copy in copies:
        copy.wait()


def shards(states, cotangents, w_conv, b_conv, w_out, forcing, land, dates):
    grad_scale = 1.0 / math.sqrt(2 * MB * TILES * ROWS * L)
    any_spec = pl.BlockSpec(memory_space=pl.ANY)
    vmem_spec = pl.BlockSpec(memory_space=pltpu.VMEM)
    dma = pltpu.SemaphoreType.DMA
    flat = (MB, C * ROWS, L)
    out, w1, w2, b1 = pl.pallas_call(
        functools.partial(kernel, grad_scale),
        out_shape=(
            pltpu.VMEM(flat, F32),
            pltpu.VMEM((18, H), F32),
            pltpu.VMEM((8, C), F32),
            pltpu.VMEM((1, L), F32),
        ),
        in_specs=[pl.BlockSpec(memory_space=pltpu.SMEM)] + [any_spec] * 7,
        out_specs=(vmem_spec, vmem_spec, vmem_spec, vmem_spec),
        scratch_shapes=[
            pltpu.VMEM(flat, F32),
            pltpu.VMEM(flat, F32),
            pltpu.VMEM((9 * C, H), BF16),
            pltpu.VMEM((H, 9 * C), BF16),
            pltpu.VMEM((3 * C, 3 * H), BF16),
            pltpu.VMEM((6 * C, H), BF16),
            pltpu.VMEM((1, H), F32),
            pltpu.VMEM((H, C), BF16),
            pltpu.VMEM(forcing.shape, F32),
            pltpu.VMEM((ROWS, L), jnp.int32),
            pltpu.VMEM((H, L), F32),
            pltpu.VMEM((MB, C, L), F32),
            pltpu.VMEM((MB, 9 * C, ROWS * L), BF16),
            pltpu.VMEM((2, MB, C, L), BF16),
            pltpu.VMEM((2, MB, C, L), BF16),
            pltpu.VMEM((MB, H, ROWS * L), BF16),
            pltpu.VMEM((MB, H, ROWS * L), F32),
            pltpu.VMEM((MB, C, ROWS * L), BF16),
            pltpu.VMEM((MB, H, (ROWS + 2) * L), BF16),
            pltpu.VMEM((H, L), F32),
            pltpu.VMEM((MB, 2, C, L), BF16),
            pltpu.VMEM((MB, 2, C, L), BF16),
            pltpu.VMEM((MB, 2, C, L), F32),
            pltpu.VMEM((MB, ROWS, C, L), BF16),
            pltpu.VMEM((MB, ROWS, C, L), BF16),
            pltpu.VMEM((9 * C, H), F32),
            pltpu.VMEM((H, C), F32),
            pltpu.VMEM((1, H), F32),
            pltpu.VMEM((BLOCKS, BROWS, 256), BF16),
            pltpu.VMEM((BLOCKS, BROWS, 256), BF16),
            pltpu.VMEM((BLOCKS, BROWS, 256), BF16),
            pltpu.VMEM((BLOCKS - 1, BROWS, 256), BF16),
            pltpu.VMEM((BROWS, 256), F32),
            pltpu.VMEM((LOCAL, 24, 256), F32),
            pltpu.VMEM((LOCAL, 24, 256), BF16),
            pltpu.VMEM((4, 24, 256), BF16),
            pltpu.VMEM((BROWS, 256), BF16),
            pltpu.VMEM((BROWS, 256), BF16),
            pltpu.VMEM((4, BLOCKS, XROWS, 256), BF16),
            pltpu.VMEM((3, BLOCKS, XROWS, 256), BF16),
            pltpu.VMEM((BLOCKS, 152, 256), F32),
            pltpu.VMEM((2, BLOCKS, 24, 256), BF16),
            pltpu.VMEM((BLOCKS, 24, 256), BF16),
            pltpu.VMEM((BLOCKS, XROWS, 256), BF16),
            pltpu.VMEM((BLOCKS, XROWS, 256), BF16),
            dma((7,)), dma((2,)), dma((2,)), dma((MB, 2)), dma((MB, 2)), dma((MB, 5)), dma((MB, 5)),
            dma((BLOCKS,)), dma((BLOCKS,)), dma((BLOCKS - 1,)), dma((BLOCKS - 1,)), dma((LOCAL, 2)), dma((4,)), dma((3,)), dma((3,)), dma((BLOCKS, 4)), dma((BLOCKS,)), dma((2,)), dma((2,)),
        ],
        compiler_params=pltpu.CompilerParams(collective_id=0, has_side_effects=True, vmem_limit_bytes=56 << 20),
    )(
        dates,
        states.reshape(flat),
        cotangents.reshape(flat),
        w_conv,
        b_conv.reshape(1, H),
        w_out,
        forcing,
        land,
    )
    out, w1, w2, b1 = pl.pallas_call(
        deliver,
        out_shape=(
            jax.ShapeDtypeStruct(flat, F32),
            jax.ShapeDtypeStruct((18, H), F32),
            jax.ShapeDtypeStruct((8, C), F32),
            jax.ShapeDtypeStruct((8,), F32),
        ),
        in_specs=[vmem_spec] * 4,
        out_specs=(any_spec,) * 4,
        scratch_shapes=[pltpu.VMEM((8,), F32), dma((4,))],
    )(*(pltpu.with_memory_space_constraint(value, pltpu.VMEM) for value in (out, w1, w2, b1)))
    return out.reshape(states.shape), w1, w2, b1


def solution(mesh):
    placed = (
        P("lead", None, None, "tile", None),
        P("lead", None, None, "tile", None),
        P(),
        P(),
        P(),
        P(),
        P("tile", None),
        P(),
    )
    return jax.shard_map(
        shards,
        mesh=mesh,
        in_specs=placed,
        out_specs=(
            P("lead", None, None, "tile", None),
            P("tile", None),
            P("tile", None),
            P("tile"),
        ),
        check_vma=False,
    )
```
